32 devices in a mesh: grp: 4 (over y, core), blk: 8 (over z, x).
Axes of the slice: x: 2, y: 2, z: 4, core: 2. Of those that a mesh axis runs over, the one named last changes fastest.
Arguments:
- rhs: float32 [1536, 1920], P(('grp', 'blk')), may hold values from -6 to 6
- membership: int32 [1536], P(('grp', 'blk')), may hold values from 0 to 7
- pair_ends: int32 [16384, 2], P(('grp', 'blk')), may hold values from 0 to 63, as said below
- pair_dir: int32 [16384], P(('grp', 'blk')), may hold values from 0 to 2
- pair_reach: float32 [16384], P(('grp', 'blk')), may hold values from 0.05 to 0.25
- pair_count: int32 [32], P(('grp', 'blk')), may hold values from 256 to 512, as said below
- send_idx: int32 [32, 14, 4], P(('grp', 'blk')), may hold values from 0 to 7
- rotation: float32 [3, 15, 128, 128], replicated, may hold values from -0.5 to 0.5
- translation: float32 [15, 128, 128], replicated, may hold values from -0.5 to 0.5
- mie: float32 [1920], replicated, may hold values from 0.2 to 1
Outputs:
- basis: float32 [1536, 1920], P(('grp', 'blk'))
- image: float32 [1536, 1920], P(('grp', 'blk'))
The draws below stay inside these ranges and needn't reach their ends.
Inputs may be any that keep to these rules, and one draw needn't show every extreme that they name: `pair_ends`: column 0 names a cluster of the pair's own device. Column 1 names either another cluster of the same device (below 8, never equal to column 0) or 8 + k * 4 + slot, the cluster sent in that slot by the neighbour at offset k, and only neighbours that lie on the grid are named. Every row of a neighbour on the grid is named by some pair among the first 256 pair slots of its device. `pair_count`: some device has all 512 pair slots live.
All inputs are finite; a program needn't handle non-finite values.
Results may differ from the reference program's by a relative error of at most 0.000053.
Values sent between devices are 32-bit elements; how exact they have to be, the bound alone decides.
A program may use at most 128 MiB of HBM per device.

```python
import math
import jax
import jax.numpy as jnp
from jax import lax

C = 1920
BK = 128
NB = 15
NDIR = 3
NPEER = 14
K_DEV = 8
P_DEV = 512
CAP = 4
S_DEV = 48
GROUPS = 4
BLOCKS = 8
NDEV = 32
ROWS_IN = 56
HALF_P = 256


def draw_pair_ends(key, part):
    base = jax.random.fold_in(key, 11)

    def one_device(index):
        device_key = jax.random.fold_in(base, index)
        key_place, key_first, key_other, key_local = jax.random.split(device_key, 4)
        device_row = index // BLOCKS
        device_col = index % BLOCKS
        offsets = jnp.arange(NPEER, dtype=jnp.int32)
        offset_f = offsets + (offsets >= 7).astype(jnp.int32)
        source_row = device_row - (offset_f // 5 - 1)
        source_col = device_col - (offset_f % 5 - 2)
        valid = (source_row >= 0) & (source_row < GROUPS) & (source_col >= 0) & (source_col < BLOCKS)
        row_valid = valid[jnp.arange(ROWS_IN, dtype=jnp.int32) // CAP]
        place = jax.random.permutation(key_place, HALF_P).astype(jnp.int32)
        ranks = jnp.zeros((HALF_P,), jnp.int32).at[place].set(jnp.arange(HALF_P, dtype=jnp.int32))
        ranks = jnp.concatenate([ranks, jnp.full((P_DEV - HALF_P,), HALF_P, jnp.int32)])
        first = jax.random.randint(key_first, (P_DEV,), 0, K_DEV, dtype=jnp.int32)
        other = jax.random.randint(key_other, (P_DEV,), 0, K_DEV + ROWS_IN - 1, dtype=jnp.int32)
        other = other + (other >= first).astype(jnp.int32)
        second = jnp.where(ranks < ROWS_IN, K_DEV + ranks, other)
        remote_pos = jnp.clip(second - K_DEV, 0, ROWS_IN - 1)
        usable = (second < K_DEV) | row_valid[remote_pos]
        step_local = jax.random.randint(key_local, (P_DEV,), 1, K_DEV, dtype=jnp.int32)
        fallback = (first + step_local) % K_DEV
        second = jnp.where(usable, second, fallback)
        return jnp.stack([first, second], axis=1)
    table = jax.vmap(one_device)(jnp.arange(NDEV, dtype=jnp.int32))
    return table.reshape(NDEV * P_DEV, 2)


def draw_pair_count(key, part):
    base = jax.random.fold_in(key, 23)
    key_counts, key_where = jax.random.split(base)
    counts = jax.random.randint(key_counts, (NDEV,), HALF_P, P_DEV + 1, dtype=jnp.int32)
    where = jax.random.randint(key_where, (), 0, NDEV, dtype=jnp.int32)
    return counts.at[where].set(P_DEV)


def with_ends(values, stream_key, smallest, top_value):
    index_at = [jax.random.randint(jax.random.fold_in(stream_key, axis), (), 0, length) for axis, length in enumerate(values.shape)]
    main_axis = values.shape.index(max(values.shape))
    next_to = index_at[:main_axis] + [(index_at[main_axis] + 1) % values.shape[main_axis]] + index_at[main_axis + 1:]
    return values.at[tuple(index_at)].set(smallest).at[tuple(next_to)].set(top_value)


def level_of(stream_key, extent, cuts, smallest, largest):
    def one(dim, parts):
        steps = jax.random.uniform(jax.random.fold_in(jax.random.fold_in(stream_key, 6), dim), (parts,), jnp.float32, smallest / len(cuts), largest / len(cuts))
        return jnp.repeat(jnp.exp(steps), extent[dim] // parts).reshape((-1,) + (1,) * (len(extent) - dim - 1))

    level = one(*cuts[0])
    for cut in cuts[1:]:
        level = level * one(*cut)
    return level


def gaussian(rng, extent, spread, reach, shards=(), kind=jnp.bfloat16):
    loudness = level_of(rng, extent, shards, -0.22, 0.18) if shards else 1.0
    values = jax.random.normal(rng, extent, jnp.float32) * spread * loudness
    return jnp.minimum(jnp.maximum(values, -reach), reach).astype(kind)


def setup_inputs(seed: int = 0) -> dict:
    key_list = jax.random.split(jax.random.key(seed), 11)
    rhs = gaussian(key_list[0], (NDEV * S_DEV, C), 1.0, 6.0, ((0, 32),), jnp.float32)
    membership = with_ends(jax.random.randint(key_list[1], (NDEV * S_DEV,), 0, K_DEV), jax.random.fold_in(key_list[1], 1), 0, K_DEV - 1).astype(jnp.int32)
    pair_ends = draw_pair_ends(jax.random.fold_in(key_list[10], 71), 0)
    pair_dir = with_ends(jax.random.randint(key_list[3], (NDEV * P_DEV,), 0, NDIR), jax.random.fold_in(key_list[3], 1), 0, NDIR - 1).astype(jnp.int32)
    pair_reach = jnp.clip(jnp.exp(math.log(0.25) - 1.609438 * jax.random.uniform(key_list[4], (NDEV * P_DEV,), jnp.float32) ** level_of(key_list[4], (NDEV * P_DEV,), ((0, 32),), -0.2, 0.2)), 0.05, 0.25)
    pair_count = draw_pair_count(jax.random.fold_in(key_list[10], 71), 0)
    send_idx = with_ends(jax.random.randint(key_list[6], (NDEV, NPEER, CAP), 0, K_DEV), jax.random.fold_in(key_list[6], 1), 0, K_DEV - 1).astype(jnp.int32)
    rotation = gaussian(key_list[7], (NDIR, NB, BK, BK), BK ** -0.5, 0.5, (), jnp.float32)
    translation = gaussian(key_list[8], (NB, BK, BK), BK ** -0.5, 0.5, (), jnp.float32)
    mie = jnp.clip(jax.random.uniform(key_list[9], (C,), jnp.float32, 0.2, 1.0), 0.2, 1.0)
    return dict(rhs=rhs, membership=membership, pair_ends=pair_ends, pair_dir=pair_dir, pair_reach=pair_reach, pair_count=pair_count, send_idx=send_idx, rotation=rotation, translation=translation, mie=mie)


HI = lax.Precision.HIGHEST

def rotate_rows(rows, rotation):
    count = rows.shape[0]
    split = rows.reshape(count, NB, BK)
    out = jnp.einsum('mgk,dgkj->mdgj', split, rotation, precision=HI)
    return out.reshape(count, NDIR, C)

def translate_frames(front, behind, translation):
    count = front.shape[0]
    half = BK // 2
    first_part = jnp.roll(front, half, axis=2).reshape(count, NDIR, NB, BK)
    second_part = jnp.roll(behind, half, axis=2).reshape(count, NDIR, NB, BK)
    out = jnp.einsum('mdgk,gkj->mdgj', first_part, translation, precision=HI)
    out = out + jnp.einsum('mdgk,gjk->mdgj', second_part, translation, precision=HI)
    return jnp.roll(out.reshape(count, NDIR, C), -half, axis=2)

def unrotate_frames(frames, rotation):
    count = frames.shape[0]
    split = frames.reshape(count, NDIR, NB, BK)
    out = jnp.einsum('mdgj,dgkj->mgk', split, rotation, precision=HI)
    return out.reshape(count, C)

def reference(rhs, membership, pair_ends, pair_dir, pair_reach, pair_count, send_idx, rotation, translation, mie):
    clusters_all = NDEV * K_DEV
    sphere_dev = (jnp.arange(NDEV * S_DEV, dtype=jnp.int32) // S_DEV).astype(jnp.int32)
    cluster_id = (sphere_dev * K_DEV + membership).astype(jnp.int32)
    pair_owner = (jnp.arange(NDEV * P_DEV, dtype=jnp.int32) // P_DEV).astype(jnp.int32)
    position = (jnp.arange(NDEV * P_DEV, dtype=jnp.int32) % P_DEV).astype(jnp.int32)
    first_end = (pair_owner * K_DEV + pair_ends[:, 0]).astype(jnp.int32)
    second = pair_ends[:, 1]
    remote_row = jnp.clip(second - K_DEV, 0, ROWS_IN - 1).astype(jnp.int32)
    offset_k = (remote_row // CAP).astype(jnp.int32)
    slot = (remote_row % CAP).astype(jnp.int32)
    offset_f = (offset_k + (offset_k >= 7).astype(jnp.int32)).astype(jnp.int32)
    row_shift = (offset_f // 5 - 1).astype(jnp.int32)
    col_shift = (offset_f % 5 - 2).astype(jnp.int32)
    owner_row = (pair_owner // BLOCKS).astype(jnp.int32)
    owner_col = (pair_owner % BLOCKS).astype(jnp.int32)
    source_row = jnp.clip(owner_row - row_shift, 0, GROUPS - 1).astype(jnp.int32)
    source_col = jnp.clip(owner_col - col_shift, 0, BLOCKS - 1).astype(jnp.int32)
    source = (source_row * BLOCKS + source_col).astype(jnp.int32)
    sent = send_idx.reshape(-1)[((source * NPEER + offset_k) * CAP + slot).astype(jnp.int32)]
    second_end = jnp.where(second >= K_DEV, source * K_DEV + sent, pair_owner * K_DEV + second).astype(jnp.int32)
    live = (position < pair_count[pair_owner]).astype(jnp.float32)
    weight = pair_reach * live
    own_index = (first_end * NDIR + pair_dir).astype(jnp.int32)
    near_index = (second_end * NDIR + pair_dir).astype(jnp.int32)

    def operator(vector):
        gathered = jax.ops.segment_sum(vector, cluster_id, num_segments=clusters_all)
        frames = rotate_rows(gathered, rotation).reshape(clusters_all * NDIR, C)
        front = jax.ops.segment_sum(weight[:, None] * frames[near_index], own_index, num_segments=clusters_all * NDIR)
        behind = jax.ops.segment_sum(weight[:, None] * frames[own_index], near_index, num_segments=clusters_all * NDIR)
        moved = translate_frames(front.reshape(clusters_all, NDIR, C), behind.reshape(clusters_all, NDIR, C), translation)
        field = unrotate_frames(moved, rotation)
        return vector - mie[None, :] * field[cluster_id]
    entries = float(NDEV * S_DEV * C)
    scale = jnp.sqrt(jnp.sum(rhs * rhs) / entries + 1e-06)
    start = rhs / scale
    first_image = operator(start)
    proj = jnp.sum(start * first_image) / entries
    rest = first_image - proj * start
    norm = jnp.sqrt(jnp.sum(rest * rest) / entries + 1e-06)
    basis = rest / norm
    return (basis, operator(basis))
```

```python
import functools

import jax
import jax.numpy as jnp
from jax import lax
from jax.experimental import pallas as pl
from jax.experimental.pallas import tpu as pltpu
from jax.sharding import PartitionSpec as P

K_DEV = 8
HI = lax.Precision.HIGHEST
MESH = pl.DeviceIdType.MESH
F32 = jnp.float32
I32 = jnp.int32
BF16 = jnp.bfloat16
LAST = (((1,), (1,)), ((), ()))
PLAIN = (((1,), (0,)), ((), ()))
BACK = PLAIN
EPS = 1e-6


def mm(a, b, dims):
    return lax.dot_general(a, b, dims, preferred_element_type=F32)


def stacked(x, axis):
    hi = x.astype(BF16).astype(F32)
    return jnp.concatenate([hi, x - hi], axis=axis).astype(BF16)


def twice(x):
    both = stacked(x, 0)
    return jnp.concatenate([both, both], axis=1)


def offsets():
    out = []
    for f in range(15):
        if f != 7:
            out.append((f // 5 - 1, f % 5 - 2))
    return out


def kernel(
    groups, blocks, ndir, nblk, entries,
    rhs_hbm, member_hbm, ends_hbm, dir_hbm, reach_hbm, count, sent_hbm, mie_hbm, rot_hbm, trans_hbm,
    coef, factor, rhs, member,
    ends, dirs, reach, sent, mie,
    rot, trans, rot_by, rot_back, tr_by, tr_back, table1, table2, frames, moved, fieldb,
    hc, part, gsum, bsum,
    wsem, send1, recv1, send2, recv2, gs, gr, bs, br,
):
    row = lax.axis_index("grp")
    col = lax.axis_index("blk")
    offs = offsets()
    npeer = len(offs)
    spheres = rhs.shape[0]
    width = 128
    K = K_DEV

    loads = [
        pltpu.make_async_copy(src, dst, wsem.at[i])
        for i, (src, dst) in enumerate([
            (rhs_hbm, rhs), (member_hbm, member), (ends_hbm, ends), (dir_hbm, dirs), (reach_hbm, reach),
            (sent_hbm, sent), (mie_hbm, mie), (rot_hbm, rot), (trans_hbm, trans),
        ])
    ]
    for load in loads:
        load.start()

    def inside(dr, dc):
        r, c = row + dr, col + dc
        return (r >= 0) & (r < groups) & (c >= 0) & (c < blocks)

    barrier = pltpu.get_barrier_semaphore()
    total = jnp.int32(groups - 1 + blocks - 1)
    for dr, dc in offs:
        ok = inside(dr, dc)
        total = total + ok.astype(jnp.int32)

        @pl.when(ok)
        def _(dr=dr, dc=dc):
            pl.semaphore_signal(barrier, inc=1, device_id=(row + dr, col + dc), device_id_type=MESH)

    for j in range(1, groups):
        pl.semaphore_signal(barrier, inc=1, device_id=(lax.rem(row + j, groups), col), device_id_type=MESH)
    for j in range(1, blocks):
        pl.semaphore_signal(barrier, inc=1, device_id=(row, lax.rem(col + j, blocks)), device_id_type=MESH)

    cap = sent.shape[0]
    for load in loads[:7]:
        load.wait()
    mem = (lax.broadcasted_iota(jnp.int32, (K, spheres), 0) == member[...]).astype(F32)
    agg = jnp.dot(mem, rhs[...], precision=HI, preferred_element_type=F32)
    for g in range(nblk):
        table1[0, ndir + g] = agg[:, g * width:(g + 1) * width]
    npairs = ends.shape[1]
    live = lax.broadcasted_iota(jnp.int32, (1, npairs), 1) < count[0]
    weight = jnp.where(live, reach[...], 0.0)
    key = dirs[...] * K + ends[0:1, :]
    left = jnp.where(lax.broadcasted_iota(jnp.int32, (ndir * K, npairs), 0) == key, weight, 0.0)
    right = (lax.broadcasted_iota(jnp.int32, (width, npairs), 0) == ends[1:2, :]).astype(F32)
    own_w = lax.dot_general(left, right, LAST, precision=HI, preferred_element_type=F32)
    at = lax.broadcasted_iota(jnp.int32, (npeer, width), 1) - (64 + K)
    peer_row = lax.broadcasted_iota(jnp.int32, (npeer, width), 0) * cap
    spread_k = jnp.where((at >= peer_row) & (at < peer_row + cap), 1.0, 0.0)
    wide = jnp.dot(sent[...].astype(F32), spread_k, precision=HI, preferred_element_type=F32)
    at4 = lax.broadcasted_iota(jnp.int32, (cap, width), 1) % cap
    row4 = lax.broadcasted_iota(jnp.int32, (cap, width), 0)
    ids = jnp.sum(jnp.where(at4 == (row4 + 64 + K) % cap, wide, 0.0), axis=0, keepdims=True)
    for d in range(ndir):
        tile = own_w[d * K:(d + 1) * K]
        table1[0, d] = tile + ids if d == 0 else tile

    for k, (dr, dc) in enumerate(offs):
        @pl.when(jnp.logical_not(inside(-dr, -dc)))
        def _(k=k):
            table1[k + 1] = jnp.zeros(table1.shape[1:], F32)
            table2[k + 1] = jnp.zeros(table2.shape[1:], F32)

    pl.semaphore_wait(barrier, total)

    def copy(table, chunk, i, k, send, recv, dr, dc):
        lo, hi = chunk
        return pltpu.make_async_remote_copy(
            src_ref=table.at[0, pl.ds(lo, hi - lo)], dst_ref=table.at[k + 1, pl.ds(lo, hi - lo)],
            send_sem=send.at[i, k], recv_sem=recv.at[i, k],
            device_id=(row + dr, col + dc), device_id_type=MESH,
        )

    def start_chunk(table, chunk, i, send, recv):
        for k, (dr, dc) in enumerate(offs):
            @pl.when(inside(dr, dc))
            def _(k=k, dr=dr, dc=dc):
                copy(table, chunk, i, k, send, recv, dr, dc).start()

    def wait_recv(table, chunk, i, send, recv):
        for k, (dr, dc) in enumerate(offs):
            @pl.when(inside(-dr, -dc))
            def _(k=k, dr=dr, dc=dc):
                copy(table, chunk, i, k, send, recv, -dr, -dc).wait_recv()

    def wait_send(table, chunk, i, send, recv):
        for k, (dr, dc) in enumerate(offs):
            @pl.when(inside(dr, dc))
            def _(k=k, dr=dr, dc=dc):
                copy(table, chunk, i, k, send, recv, dr, dc).wait_send()

    third = nblk // 3
    first_blocks = [list(range(0, third)), list(range(third, 2 * third)), list(range(2 * third, nblk))]
    second_blocks = [
        list(range(1, third - 1)), list(range(third - 1, 2 * third - 1)),
        list(range(2 * third - 1, nblk)) + [0],
    ]

    def spans(groups_of, lead):
        out, pos = [], 0
        for blocks_of in groups_of:
            end = pos + len(blocks_of) + (lead if not out else 0)
            out.append((pos, end))
            pos = end
        return out

    chunks1, chunks2 = spans(first_blocks, ndir), spans(second_blocks, 0)
    at1 = {g: g + ndir for g in range(nblk)}
    at2 = {g: (g - 1) % nblk for g in range(nblk)}
    for i, chunk in enumerate(chunks1):
        start_chunk(table1, chunk, i, send1, recv1)

    squares = jnp.zeros((K, width), F32)
    for g in range(nblk):
        for s in range(0, spheres, K):
            v = rhs[s:s + K, g * width:(g + 1) * width]
            squares = squares + v * v
    counts = jnp.sum(mem, axis=1, keepdims=True)
    for load in loads[7:]:
        load.wait()
    for g in range(nblk):
        for d in range(ndir):
            rot_by[d, g] = stacked(rot[d, g], 0)
            rot_back[d, g] = stacked(rot[d, g].T, 0)
        tr_by[g] = stacked(trans[g], 0)
        tr_back[g] = stacked(trans[g].T, 0)
    wait_recv(table1, chunks1[0], 0, send1, recv1)

    rows = (npeer + 1) * K
    lane = lax.broadcasted_iota(jnp.int32, (rows, width), 1)
    sub = lax.broadcasted_iota(jnp.int32, (rows, width), 0)
    slot = sub // K
    lane8 = lax.broadcasted_iota(jnp.int32, (K, width), 1)
    far = jnp.zeros((K, width), F32)
    for k in range(npeer):
        first = 64 + K + cap * k
        far = far + jnp.where((lane8 >= first) & (lane8 < first + cap), table1[k + 1, 0], 0.0)
    far = pltpu.roll(far, 64, 1)
    far = jnp.broadcast_to(far[0:1], (rows, width))
    low = K + cap * (slot - 1)
    subk = (sub % K)
    wanted = jnp.where(lane < K, subk.astype(F32), far)
    lane_key = jnp.where(lane < K, lane.astype(F32), subk.astype(F32))
    begin = jnp.where(slot == 0, 0, low)
    end = jnp.where(slot == 0, K, low + cap)
    pick = jnp.where((lane >= begin) & (lane < end) & (wanted == lane_key), 1.0, 0.0)
    mine = pltpu.roll(jnp.broadcast_to(ids, (K, width)), 64, 1)
    sub8 = lax.broadcasted_iota(jnp.int32, (K, width), 0)
    named = jnp.where(lane8 < K, lane8.astype(F32), mine)
    take = jnp.where((lane8 < 64) & (named == sub8.astype(F32)), 1.0, 0.0)
    back = K + cap * (npeer - slot)
    start = jnp.where(slot == 0, 0, back)
    stop = jnp.where(slot == 0, K, back + cap)
    keep = (lane >= start) & (lane < stop)
    front_w, behind_w = [], []
    for d in range(ndir):
        front_w.append(lax.dot_general(
            jnp.where(lane8 < 64, table1[0, d], 0.0), pick, LAST, precision=HI,
            preferred_element_type=F32))
        every = jnp.where(keep, table1[:, d].reshape(rows, width), 0.0)
        behind_w.append(lax.dot_general(take, every, LAST, precision=HI, preferred_element_type=F32))
    wts = jnp.concatenate(front_w + behind_w, axis=0)
    n_all = wts.shape[0]
    pad = jnp.zeros((width - rows, width), F32)
    w_both = twice(jnp.concatenate([wts, jnp.zeros((n_all, width - rows), F32)], axis=1))

    lanes = lax.broadcasted_iota(jnp.int32, (ndir * K, width), 1)
    lanes2 = lax.broadcasted_iota(jnp.int32, (2 * ndir * K, width), 1)
    nd = ndir * K

    def products(jobs):
        both = [twice(x) for x, _, _ in jobs]
        tops = [mm(b, w, dims) for b, (_, w, dims) in zip(both, jobs)]
        return [t[:t.shape[0] // 2] + t[t.shape[0] // 2:] for t in tops]

    def frame_steps(table, place, gs):
        tabs = [stacked(jnp.concatenate([table[:, place[g]].reshape(rows, width), pad], axis=0), 0) for g in gs]
        tops = [mm(w_both, t, PLAIN) for t in tabs]
        jobs = []
        for g, top in zip(gs, tops):
            mix = top[:n_all] + top[n_all:]
            for d in range(ndir):
                x = jnp.concatenate([mix[d * K:(d + 1) * K], mix[nd + d * K:nd + (d + 1) * K]], axis=0)
                jobs.append((x, rot_by[d, g], PLAIN))
        ys = products(jobs)
        for i, g in enumerate(gs):
            y = ys[i * ndir:(i + 1) * ndir]
            frames[g] = pltpu.roll(jnp.concatenate([t[:K] for t in y] + [t[K:] for t in y], axis=0), 64, 1)

    def move_steps(gs):
        jobs = []
        for g in gs:
            x = jnp.where(lanes2 < 64, frames[(g - 1) % nblk], frames[g])
            jobs.append((x[:nd], tr_by[g], PLAIN))
            jobs.append((x[nd:], tr_back[g], BACK))
        ys = products(jobs)
        for i, g in enumerate(gs):
            moved[g] = pltpu.roll(ys[2 * i] + ys[2 * i + 1], 64, 1)

    def field_steps(gs):
        jobs = []
        for g in gs:
            u = jnp.where(lanes < 64, moved[g], moved[(g + 1) % nblk])
            for d in range(ndir):
                jobs.append((u[d * K:(d + 1) * K], rot_back[d, g], BACK))
        ys = products(jobs)
        for i, g in enumerate(gs):
            acc = ys[i * ndir]
            for d in range(1, ndir):
                acc = acc + ys[i * ndir + d]
            fieldb[g] = acc * mie[g:g + 1, :]

    def field_of(table, place, blocks_in, before, after):
        have_f, have_u, have_h = set(), set(), set()
        for i, new in enumerate(blocks_in):
            before(i)
            frame_steps(table, place, new)
            have_f |= set(new)
            ready = [g for g in range(nblk) if g not in have_u and g in have_f and (g - 1) % nblk in have_f]
            move_steps(ready)
            have_u |= set(ready)
            ready = [g for g in range(nblk) if g not in have_h and g in have_u and (g + 1) % nblk in have_u]
            field_steps(ready)
            have_h |= set(ready)
            after(i, have_h)

    def line_copy(j, source, sums, send, recv, axis):
        here, size = (row, groups) if axis == 0 else (col, blocks)
        peer = lax.rem(here + j, size)
        return pltpu.make_async_remote_copy(
            src_ref=source, dst_ref=sums.at[here],
            send_sem=send.at[j - 1], recv_sem=recv.at[j - 1],
            device_id=(peer, col) if axis == 0 else (row, peer), device_id_type=MESH,
        )

    def line_wait(j, source, sums, recv, send, axis):
        here, size = (row, groups) if axis == 0 else (col, blocks)
        peer = lax.rem(here + size - j, size)
        pltpu.make_async_remote_copy(
            src_ref=source, dst_ref=sums.at[peer],
            send_sem=send.at[j - 1], recv_sem=recv.at[j - 1],
            device_id=(peer, col) if axis == 0 else (row, peer), device_id_type=MESH,
        ).wait_recv()

    sums_in = [jnp.zeros((K, width), F32), jnp.zeros((K, width), F32)]

    def before1(i):
        if i:
            wait_recv(table1, chunks1[i], i, send1, recv1)

    def after1(i, have):
        assert set(second_blocks[i]) <= have
        for g in second_blocks[i]:
            h = fieldb[g]
            hc[g] = h
            scaled = h * counts
            table2[0, at2[g]] = scaled
            sums_in[0] = sums_in[0] + h * table1[0, at1[g]]
            sums_in[1] = sums_in[1] + h * scaled
        if i == 2:
            fold = lambda t: jnp.sum(t, axis=0, keepdims=True)
            zero = jnp.zeros((K - 3, width), F32)
            mine_part = jnp.concatenate([fold(squares), fold(sums_in[0]), fold(sums_in[1]), zero], axis=0)
            part[...] = mine_part
            gsum[row] = mine_part
            for j in range(1, groups):
                line_copy(j, part, gsum, gs, gr, 0).start()
        start_chunk(table2, chunks2[i], i, send2, recv2)

    field_of(table1, at1, first_blocks, before1, after1)

    def before2(i):
        wait_recv(table2, chunks2[i], i, send2, recv2)
        if i == 1:
            for j in range(1, groups):
                line_wait(j, part, gsum, gr, gs, 0)
            for j in range(1, groups):
                line_copy(j, part, gsum, gs, gr, 0).wait_send()
            line = gsum[0]
            for j in range(1, groups):
                line = line + gsum[j]
            part[...] = line
            bsum[col] = line
            for j in range(1, blocks):
                line_copy(j, part, bsum, bs, br, 1).start()

    field_of(table2, at2, second_blocks, before2, lambda i, have: None)

    for j in range(1, blocks):
        line_wait(j, part, bsum, br, bs, 1)
    for j in range(1, blocks):
        line_copy(j, part, bsum, bs, br, 1).wait_send()
    sums = bsum[0]
    for j in range(1, blocks):
        sums = sums + bsum[j]
    sums = jnp.sum(sums, axis=1, keepdims=True)
    s_, a_, b_ = sums[0:1], sums[1:2], sums[2:3]
    shift = entries * EPS
    q = (a_ + shift) / (s_ + shift)
    scale2 = (s_ + shift) / entries
    norm2 = (q * q * s_ - 2.0 * q * a_ + b_) / (entries * scale2) + EPS
    inv = 1.0 / jnp.sqrt(scale2 * norm2)
    for g in range(nblk):
        span = slice(g * width, (g + 1) * width)
        h = hc[g]
        coef[:K, span] = h * inv
        coef[K:, span] = (q * h - fieldb[g]) * inv
    factor[...] = jnp.broadcast_to(q * inv, factor.shape)

    for i in range(3):
        wait_send(table1, chunks1[i], i, send1, recv1)
        wait_send(table2, chunks2[i], i, send2, recv2)


def closing(coef, factor, rhs, member, basis, image):
    spheres, full = rhs.shape
    mem = (lax.broadcasted_iota(I32, (K_DEV, spheres), 0) == member[...]).astype(BF16)
    mem3 = jnp.concatenate([mem.astype(F32)] * 3, axis=0).astype(BF16)
    scale = factor[0:1, 0:1]
    dims = (((0,), (0,)), ((), ()))

    def spread(x):
        hi = x.astype(BF16).astype(F32)
        mid = (x - hi).astype(BF16).astype(F32)
        return mm(mem3, jnp.concatenate([hi, mid, x - hi - mid], axis=0).astype(BF16), dims)

    out = rhs[...] * scale - spread(coef[:K_DEV, :])
    basis[...] = out
    image[...] = out - spread(coef[K_DEV:, :])


def body(rhs, membership, pair_ends, pair_dir, pair_reach, pair_count, send_idx, rotation, translation, mie):
    groups, blocks = lax.axis_size("grp"), lax.axis_size("blk")
    spheres, full = rhs.shape
    ndir, nblk, width = rotation.shape[:3]
    npeer, cap = send_idx.shape[1:]
    npairs = pair_dir.shape[0]
    K = K_DEV
    vm = pl.BlockSpec(memory_space=pltpu.VMEM)
    hb = pl.BlockSpec(memory_space=pl.ANY)
    V, D = pltpu.VMEM, pltpu.SemaphoreType.DMA
    out = jax.ShapeDtypeStruct(rhs.shape, F32)
    entries = float(groups * blocks * spheres * full)
    parts = pl.pallas_call(
        functools.partial(kernel, groups, blocks, ndir, nblk, entries),
        out_shape=(V((2 * K, full), F32), V((K, width), F32), V(rhs.shape, F32), V((1, spheres), I32)),
        in_specs=[hb] * 5 + [pl.BlockSpec(memory_space=pltpu.SMEM)] + [hb] * 4,
        out_specs=(vm,) * 4,
        scratch_shapes=[
            V((2, npairs), I32), V((1, npairs), I32), V((1, npairs), F32), V((cap, npeer), I32), V((nblk, width), F32),
            V(rotation.shape, F32), V(translation.shape, F32),
            V((ndir, nblk, 2 * width, width), BF16), V((ndir, nblk, 2 * width, width), BF16),
            V((nblk, 2 * width, width), BF16), V((nblk, 2 * width, width), BF16),
            V((npeer + 1, nblk + ndir, K, width), F32), V((npeer + 1, nblk, K, width), F32),
            V((nblk, 2 * ndir * K, width), F32), V((nblk, ndir * K, width), F32), V((nblk, K, width), F32),
            V((nblk, K, width), F32), V((K, width), F32), V((groups, K, width), F32), V((blocks, K, width), F32),
            D((9,)), D((3, npeer)), D((3, npeer)), D((3, npeer)), D((3, npeer)),
            D((groups - 1,)), D((groups - 1,)), D((blocks - 1,)), D((blocks - 1,)),
        ],
        compiler_params=pltpu.CompilerParams(
            collective_id=0, has_side_effects=True, vmem_limit_bytes=48 << 20
        ),
    )(*[x if x.size == 1 else pltpu.with_memory_space_constraint(x, pltpu.HBM) for x in (
        rhs, membership[None, :], pair_ends.T, pair_dir[None, :], pair_reach[None, :], pair_count,
        send_idx[0].T, mie.reshape(nblk, width), rotation, translation,
    )])
    return pl.pallas_call(
        closing,
        out_shape=(out, out),
        in_specs=[vm] * 4,
        out_specs=(vm, vm),
        compiler_params=pltpu.CompilerParams(vmem_limit_bytes=8 << 20),
    )(*parts)


def solution(mesh):
    both = ("grp", "blk")
    placed = (
        P(both, None), P(both), P(both, None), P(both), P(both), P(both), P(both, None, None), P(), P(), P(),
    )
    return jax.shard_map(
        body, mesh=mesh, in_specs=placed, out_specs=(P(both, None), P(both, None)), check_vma=False
    )
```

```python
import functools

import jax
import jax.numpy as jnp
from jax import lax
from jax.experimental import pallas as pl
from jax.experimental.pallas import tpu as pltpu
from jax.sharding import PartitionSpec as P

K_DEV = 8
HI = lax.Precision.HIGHEST
MESH = pl.DeviceIdType.MESH
F32 = jnp.float32
I32 = jnp.int32
BF16 = jnp.bfloat16
LAST = (((1,), (1,)), ((), ()))
PLAIN = (((1,), (0,)), ((), ()))
BACK = PLAIN
EPS = 1e-6


def mm(a, b, dims):
    return lax.dot_general(a, b, dims, preferred_element_type=F32)


def stacked(x, axis):
    hi = x.astype(BF16).astype(F32)
    return jnp.concatenate([hi, x - hi], axis=axis).astype(BF16)


def twice(x):
    both = stacked(x, 0)
    return jnp.concatenate([both, both], axis=1)


def offsets():
    out = []
    for f in range(15):
        if f != 7:
            out.append((f // 5 - 1, f % 5 - 2))
    return out


def kernel(
    groups, blocks, ndir, nblk, entries,
    rhs_hbm, member_hbm, ends_hbm, dir_hbm, reach_hbm, count, sent_hbm, mie_hbm, rot_hbm, trans_hbm,
    coef, factor, rhs, member,
    ends, dirs, reach, sent, mie,
    rot, trans, rot_by, rot_back, tr_by, tr_back, table1, table2, frames, moved, fieldb,
    hc, part, gsum, bsum,
    wsem, send1, recv1, send2, recv2, gs, gr, bs, br,
):
    row = lax.axis_index("grp")
    col = lax.axis_index("blk")
    offs = offsets()
    npeer = len(offs)
    spheres = rhs.shape[0]
    width = 128
    K = K_DEV

    loads = [
        pltpu.make_async_copy(src, dst, wsem.at[i])
        for i, (src, dst) in enumerate([
            (rhs_hbm, rhs), (member_hbm, member), (ends_hbm, ends), (dir_hbm, dirs), (reach_hbm, reach),
            (sent_hbm, sent), (mie_hbm, mie), (rot_hbm, rot), (trans_hbm, trans),
        ])
    ]
    for load in loads:
        load.start()

    partner = 1 - 2 * lax.rem(row, 2)
    other = -partner

    def inside(dr, dc):
        r, c = row + dr, col + dc
        return (r >= 0) & (r < groups) & (c >= 0) & (c < blocks)

    barrier = pltpu.get_barrier_semaphore()
    total = jnp.int32(groups - 1 + blocks - 1)
    for dc in (-2, -1, 1, 2):
        ok = inside(other, dc)
        total = total + ok.astype(jnp.int32)

        @pl.when(ok)
        def _(dc=dc):
            pl.semaphore_signal(barrier, inc=1, device_id=(row + other, col + dc), device_id_type=MESH)

    for j in range(1, groups):
        pl.semaphore_signal(barrier, inc=1, device_id=(lax.rem(row + j, groups), col), device_id_type=MESH)
    for j in range(1, blocks):
        pl.semaphore_signal(barrier, inc=1, device_id=(row, lax.rem(col + j, blocks)), device_id_type=MESH)

    cap = sent.shape[0]
    for load in loads[:7]:
        load.wait()
    mem = (lax.broadcasted_iota(jnp.int32, (K, spheres), 0) == member[...]).astype(F32)
    agg = jnp.dot(mem, rhs[...], precision=HI, preferred_element_type=F32)
    for g in range(nblk):
        table1[0, ndir + g] = agg[:, g * width:(g + 1) * width]
    npairs = ends.shape[1]
    live = lax.broadcasted_iota(jnp.int32, (1, npairs), 1) < count[0]
    weight = jnp.where(live, reach[...], 0.0)
    key = dirs[...] * K + ends[0:1, :]
    left = jnp.where(lax.broadcasted_iota(jnp.int32, (ndir * K, npairs), 0) == key, weight, 0.0)
    right = (lax.broadcasted_iota(jnp.int32, (width, npairs), 0) == ends[1:2, :]).astype(F32)
    own_w = lax.dot_general(left, right, LAST, precision=HI, preferred_element_type=F32)
    at = lax.broadcasted_iota(jnp.int32, (npeer, width), 1) - (64 + K)
    peer_row = lax.broadcasted_iota(jnp.int32, (npeer, width), 0) * cap
    spread_k = jnp.where((at >= peer_row) & (at < peer_row + cap), 1.0, 0.0)
    wide = jnp.dot(sent[...].astype(F32), spread_k, precision=HI, preferred_element_type=F32)
    at4 = lax.broadcasted_iota(jnp.int32, (cap, width), 1) % cap
    row4 = lax.broadcasted_iota(jnp.int32, (cap, width), 0)
    ids = jnp.sum(jnp.where(at4 == (row4 + 64 + K) % cap, wide, 0.0), axis=0, keepdims=True)
    for d in range(ndir):
        tile = own_w[d * K:(d + 1) * K]
        table1[0, d] = tile + ids if d == 0 else tile

    for k, (dr, dc) in enumerate(offs):
        @pl.when(jnp.logical_not(inside(-dr, -dc)))
        def _(k=k):
            table1[k + 1] = jnp.zeros(table1.shape[1:], F32)
            table2[k + 1] = jnp.zeros(table2.shape[1:], F32)

    pl.semaphore_wait(barrier, total)

    half = len(offs) // 2
    near = (-2, 2, -1, 1)

    def slot_of(dr, dc):
        return 3 + dc + (half + 2) * ((dr + 1) // 2)

    def copy(table, chunk, i, way, dc, send, recv, to):
        lo, hi = chunk
        if way == 0:
            held, slot, dr, go = 0, half + dc + (dc < 0), 0, dc
        elif way == 1:
            held = 0 if dc == 0 else half + dc + (dc < 0)
            slot, dr, go = slot_of(to * partner, dc), partner, 0
        else:
            held, slot, dr, go = 0, slot_of(to * other, dc), other, dc
        return pltpu.make_async_remote_copy(
            src_ref=table.at[held, pl.ds(lo, hi - lo)], dst_ref=table.at[slot, pl.ds(lo, hi - lo)],
            send_sem=send.at[i, 5 * way + dc + 2], recv_sem=recv.at[i, 5 * way + dc + 2],
            device_id=(row + dr, col + to * go), device_id_type=MESH,
        )

    def sends(way, dc):
        return inside(0, dc) if way == 0 else inside(partner, -dc) if way == 1 else inside(other, dc)

    def takes(way, dc):
        return inside((0, partner, other)[way], -dc)

    everything = [(0, dc) for dc in near] + [(1, dc) for dc in (0,) + near] + [(2, dc) for dc in (0,) + near]
    direct = [(1, 0)] + [(0, dc) for dc in near] + [(2, dc) for dc in near + (0,)]

    def start_some(table, chunk, i, send, recv, which):
        for way, dc in which:
            @pl.when(sends(way, dc))
            def _(way=way, dc=dc):
                copy(table, chunk, i, way, dc, send, recv, 1).start()

    def start_chunk(table, chunk, i, send, recv):
        start_some(table, chunk, i, send, recv, direct)

    def wait_some(table, chunk, i, send, recv, which):
        for way, dc in which:
            @pl.when(takes(way, dc))
            def _(way=way, dc=dc):
                copy(table, chunk, i, way, dc, send, recv, -1).wait_recv()

    def wait_send(table, chunk, i, send, recv):
        for way, dc in everything:
            @pl.when(sends(way, dc))
            def _(way=way, dc=dc):
                copy(table, chunk, i, way, dc, send, recv, 1).wait_send()

    def pass_on(table, chunk, i, send, recv):
        for dc in near:
            wait_some(table, chunk, i, send, recv, [(0, dc)])
            start_some(table, chunk, i, send, recv, [(1, dc)])

    def wait_rest(table, chunk, i, send, recv):
        wait_some(table, chunk, i, send, recv, [w for w in everything if w[0]])

    cuts = [0] + [nblk * c // 15 for c in (8,)] + [nblk]
    parts = len(cuts) - 1
    first_blocks = [list(range(a, b)) for a, b in zip(cuts, cuts[1:])]
    second_blocks = [list(range(max(a - 1, 1), b - 1)) for a, b in zip(cuts, cuts[1:])]
    second_blocks[-1] += [nblk - 1, 0]

    def spans(groups_of, lead):
        out, pos = [], 0
        for blocks_of in groups_of:
            end = pos + len(blocks_of) + (lead if not out else 0)
            out.append((pos, end))
            pos = end
        return out

    chunks1, chunks2 = spans(first_blocks, ndir), spans(second_blocks, 0)
    at1 = {g: g + ndir for g in range(nblk)}
    at2 = {g: (g - 1) % nblk for g in range(nblk)}
    ahead = 1

    def ready(table, chunks, i, send, recv):
        for j in range(ahead + 1) if i == 0 else [i + ahead]:
            if j < parts:
                pass_on(table, chunks[j], j, send, recv)
        wait_rest(table, chunks[i], i, send, recv)

    for i, chunk in enumerate(chunks1):
        start_chunk(table1, chunk, i, send1, recv1)

    squares = jnp.zeros((K, width), F32)
    for g in range(nblk):
        for s in range(0, spheres, K):
            v = rhs[s:s + K, g * width:(g + 1) * width]
            squares = squares + v * v
    counts = jnp.sum(mem, axis=1, keepdims=True)
    for load in loads[7:]:
        load.wait()
    for g in range(nblk):
        for d in range(ndir):
            rot_by[d, g] = stacked(rot[d, g], 0)
            rot_back[d, g] = stacked(rot[d, g].T, 0)
        tr_by[g] = stacked(trans[g], 0)
        tr_back[g] = stacked(trans[g].T, 0)
    ready(table1, chunks1, 0, send1, recv1)

    rows = (npeer + 1) * K
    lane = lax.broadcasted_iota(jnp.int32, (rows, width), 1)
    sub = lax.broadcasted_iota(jnp.int32, (rows, width), 0)
    slot = sub // K
    lane8 = lax.broadcasted_iota(jnp.int32, (K, width), 1)
    far = jnp.zeros((K, width), F32)
    for k in range(npeer):
        first = 64 + K + cap * k
        far = far + jnp.where((lane8 >= first) & (lane8 < first + cap), table1[k + 1, 0], 0.0)
    far = pltpu.roll(far, 64, 1)
    far = jnp.broadcast_to(far[0:1], (rows, width))
    low = K + cap * (slot - 1)
    subk = (sub % K)
    wanted = jnp.where(lane < K, subk.astype(F32), far)
    lane_key = jnp.where(lane < K, lane.astype(F32), subk.astype(F32))
    begin = jnp.where(slot == 0, 0, low)
    end = jnp.where(slot == 0, K, low + cap)
    pick = jnp.where((lane >= begin) & (lane < end) & (wanted == lane_key), 1.0, 0.0)
    mine = pltpu.roll(jnp.broadcast_to(ids, (K, width)), 64, 1)
    sub8 = lax.broadcasted_iota(jnp.int32, (K, width), 0)
    named = jnp.where(lane8 < K, lane8.astype(F32), mine)
    take = jnp.where((lane8 < 64) & (named == sub8.astype(F32)), 1.0, 0.0)
    back = K + cap * (npeer - slot)
    start = jnp.where(slot == 0, 0, back)
    stop = jnp.where(slot == 0, K, back + cap)
    keep = (lane >= start) & (lane < stop)
    front_w, behind_w = [], []
    for d in range(ndir):
        front_w.append(lax.dot_general(
            jnp.where(lane8 < 64, table1[0, d], 0.0), pick, LAST, precision=HI,
            preferred_element_type=F32))
        every = jnp.where(keep, table1[:, d].reshape(rows, width), 0.0)
        behind_w.append(lax.dot_general(take, every, LAST, precision=HI, preferred_element_type=F32))
    wts = jnp.concatenate(front_w + behind_w, axis=0)
    n_all = wts.shape[0]
    pad = jnp.zeros((width - rows, width), F32)
    w_both = twice(jnp.concatenate([wts, jnp.zeros((n_all, width - rows), F32)], axis=1))

    lanes = lax.broadcasted_iota(jnp.int32, (ndir * K, width), 1)
    lanes2 = lax.broadcasted_iota(jnp.int32, (2 * ndir * K, width), 1)
    nd = ndir * K

    def products(jobs):
        both = [twice(x) for x, _, _ in jobs]
        tops = [mm(b, w, dims) for b, (_, w, dims) in zip(both, jobs)]
        return [t[:t.shape[0] // 2] + t[t.shape[0] // 2:] for t in tops]

    def frame_steps(table, place, gs):
        tabs = [stacked(jnp.concatenate([table[:, place[g]].reshape(rows, width), pad], axis=0), 0) for g in gs]
        tops = [mm(w_both, t, PLAIN) for t in tabs]
        jobs = []
        for g, top in zip(gs, tops):
            mix = top[:n_all] + top[n_all:]
            for d in range(ndir):
                x = jnp.concatenate([mix[d * K:(d + 1) * K], mix[nd + d * K:nd + (d + 1) * K]], axis=0)
                jobs.append((x, rot_by[d, g], PLAIN))
        ys = products(jobs)
        for i, g in enumerate(gs):
            y = ys[i * ndir:(i + 1) * ndir]
            frames[g] = pltpu.roll(jnp.concatenate([t[:K] for t in y] + [t[K:] for t in y], axis=0), 64, 1)

    def move_steps(gs):
        jobs = []
        for g in gs:
            x = jnp.where(lanes2 < 64, frames[(g - 1) % nblk], frames[g])
            jobs.append((x[:nd], tr_by[g], PLAIN))
            jobs.append((x[nd:], tr_back[g], BACK))
        ys = products(jobs)
        for i, g in enumerate(gs):
            moved[g] = pltpu.roll(ys[2 * i] + ys[2 * i + 1], 64, 1)

    def field_steps(gs):
        jobs = []
        for g in gs:
            u = jnp.where(lanes < 64, moved[g], moved[(g + 1) % nblk])
            for d in range(ndir):
                jobs.append((u[d * K:(d + 1) * K], rot_back[d, g], BACK))
        ys = products(jobs)
        for i, g in enumerate(gs):
            acc = ys[i * ndir]
            for d in range(1, ndir):
                acc = acc + ys[i * ndir + d]
            fieldb[g] = acc * mie[g:g + 1, :]

    def field_of(table, place, blocks_in, before, after):
        have_f, have_u, have_h = set(), set(), set()
        for i, new in enumerate(blocks_in):
            before(i)
            frame_steps(table, place, new)
            have_f |= set(new)
            ready = [g for g in range(nblk) if g not in have_u and g in have_f and (g - 1) % nblk in have_f]
            move_steps(ready)
            have_u |= set(ready)
            ready = [g for g in range(nblk) if g not in have_h and g in have_u and (g + 1) % nblk in have_u]
            field_steps(ready)
            have_h |= set(ready)
            after(i, have_h)

    def line_copy(j, source, sums, send, recv, axis):
        here, size = (row, groups) if axis == 0 else (col, blocks)
        peer = lax.rem(here + j, size)
        return pltpu.make_async_remote_copy(
            src_ref=source, dst_ref=sums.at[here],
            send_sem=send.at[j - 1], recv_sem=recv.at[j - 1],
            device_id=(peer, col) if axis == 0 else (row, peer), device_id_type=MESH,
        )

    def line_wait(j, source, sums, recv, send, axis):
        here, size = (row, groups) if axis == 0 else (col, blocks)
        peer = lax.rem(here + size - j, size)
        pltpu.make_async_remote_copy(
            src_ref=source, dst_ref=sums.at[peer],
            send_sem=send.at[j - 1], recv_sem=recv.at[j - 1],
            device_id=(peer, col) if axis == 0 else (row, peer), device_id_type=MESH,
        ).wait_recv()

    sums_in = [jnp.zeros((K, width), F32), jnp.zeros((K, width), F32)]

    def before1(i):
        if i:
            ready(table1, chunks1, i, send1, recv1)

    def after1(i, have):
        assert set(second_blocks[i]) <= have
        for g in second_blocks[i]:
            h = fieldb[g]
            hc[g] = h
            scaled = h * counts
            table2[0, at2[g]] = scaled
            sums_in[0] = sums_in[0] + h * table1[0, at1[g]]
            sums_in[1] = sums_in[1] + h * scaled
        if i == parts - 1:
            fold = lambda t: jnp.sum(t, axis=0, keepdims=True)
            zero = jnp.zeros((K - 3, width), F32)
            mine_part = jnp.concatenate([fold(squares), fold(sums_in[0]), fold(sums_in[1]), zero], axis=0)
            part[...] = mine_part
            gsum[row] = mine_part
            for j in range(1, groups):
                line_copy(j, part, gsum, gs, gr, 0).start()
        start_chunk(table2, chunks2[i], i, send2, recv2)

    field_of(table1, at1, first_blocks, before1, after1)

    def before2(i):
        if i == parts - 1:
            for j in range(parts):
                wait_send(table1, chunks1[j], j, send1, recv1)
        if i == 0:
            for j in range(1, groups):
                line_wait(j, part, gsum, gr, gs, 0)
            for j in range(1, groups):
                line_copy(j, part, gsum, gs, gr, 0).wait_send()
            line = gsum[0]
            for j in range(1, groups):
                line = line + gsum[j]
            part[...] = line
            bsum[col] = line
            for j in range(1, blocks):
                line_copy(j, part, bsum, bs, br, 1).start()
        ready(table2, chunks2, i, send2, recv2)

    field_of(table2, at2, second_blocks, before2, lambda i, have: None)

    for j in range(1, blocks):
        line_wait(j, part, bsum, br, bs, 1)
    for j in range(1, blocks):
        line_copy(j, part, bsum, bs, br, 1).wait_send()
    sums = bsum[0]
    for j in range(1, blocks):
        sums = sums + bsum[j]
    sums = jnp.sum(sums, axis=1, keepdims=True)
    s_, a_, b_ = sums[0:1], sums[1:2], sums[2:3]
    shift = entries * EPS
    q = (a_ + shift) / (s_ + shift)
    scale2 = (s_ + shift) / entries
    norm2 = (q * q * s_ - 2.0 * q * a_ + b_) / (entries * scale2) + EPS
    inv = 1.0 / jnp.sqrt(scale2 * norm2)
    for g in range(nblk):
        span = slice(g * width, (g + 1) * width)
        h = hc[g]
        coef[:K, span] = h * inv
        coef[K:, span] = (q * h - fieldb[g]) * inv
    factor[...] = jnp.broadcast_to(q * inv, factor.shape)

    for i in range(parts):
        wait_send(table2, chunks2[i], i, send2, recv2)


def closing(coef, factor, rhs, member, basis, image):
    spheres, full = rhs.shape
    mem = (lax.broadcasted_iota(I32, (K_DEV, spheres), 0) == member[...]).astype(BF16)
    mem3 = jnp.concatenate([mem.astype(F32)] * 3, axis=0).astype(BF16)
    scale = factor[0:1, 0:1]
    dims = (((0,), (0,)), ((), ()))

    def spread(x):
        hi = x.astype(BF16).astype(F32)
        mid = (x - hi).astype(BF16).astype(F32)
        return mm(mem3, jnp.concatenate([hi, mid, x - hi - mid], axis=0).astype(BF16), dims)

    out = rhs[...] * scale - spread(coef[:K_DEV, :])
    basis[...] = out
    image[...] = out - spread(coef[K_DEV:, :])


def body(rhs, membership, pair_ends, pair_dir, pair_reach, pair_count, send_idx, rotation, translation, mie):
    groups, blocks = lax.axis_size("grp"), lax.axis_size("blk")
    spheres, full = rhs.shape
    ndir, nblk, width = rotation.shape[:3]
    npeer, cap = send_idx.shape[1:]
    npairs = pair_dir.shape[0]
    K = K_DEV
    vm = pl.BlockSpec(memory_space=pltpu.VMEM)
    hb = pl.BlockSpec(memory_space=pl.ANY)
    V, D = pltpu.VMEM, pltpu.SemaphoreType.DMA
    out = jax.ShapeDtypeStruct(rhs.shape, F32)
    entries = float(groups * blocks * spheres * full)
    parts = pl.pallas_call(
        functools.partial(kernel, groups, blocks, ndir, nblk, entries),
        out_shape=(V((2 * K, full), F32), V((K, width), F32), V(rhs.shape, F32), V((1, spheres), I32)),
        in_specs=[hb] * 5 + [pl.BlockSpec(memory_space=pltpu.SMEM)] + [hb] * 4,
        out_specs=(vm,) * 4,
        scratch_shapes=[
            V((2, npairs), I32), V((1, npairs), I32), V((1, npairs), F32), V((cap, npeer), I32), V((nblk, width), F32),
            V(rotation.shape, F32), V(translation.shape, F32),
            V((ndir, nblk, 2 * width, width), BF16), V((ndir, nblk, 2 * width, width), BF16),
            V((nblk, 2 * width, width), BF16), V((nblk, 2 * width, width), BF16),
            V((npeer + 1, nblk + ndir, K, width), F32), V((npeer + 1, nblk, K, width), F32),
            V((nblk, 2 * ndir * K, width), F32), V((nblk, ndir * K, width), F32), V((nblk, K, width), F32),
            V((nblk, K, width), F32), V((K, width), F32), V((groups, K, width), F32), V((blocks, K, width), F32),
            D((9,)), D((2, 15)), D((2, 15)), D((2, 15)), D((2, 15)),
            D((groups - 1,)), D((groups - 1,)), D((blocks - 1,)), D((blocks - 1,)),
        ],
        compiler_params=pltpu.CompilerParams(
            collective_id=0, has_side_effects=True, vmem_limit_bytes=48 << 20
        ),
    )(*[x if x.size == 1 else pltpu.with_memory_space_constraint(x, pltpu.HBM) for x in (
        rhs, membership[None, :], pair_ends.T, pair_dir[None, :], pair_reach[None, :], pair_count,
        send_idx[0].T, mie.reshape(nblk, width), rotation, translation,
    )])
    return pl.pallas_call(
        closing,
        out_shape=(out, out),
        in_specs=[vm] * 4,
        out_specs=(vm, vm),
        compiler_params=pltpu.CompilerParams(vmem_limit_bytes=8 << 20),
    )(*parts)


def solution(mesh):
    both = ("grp", "blk")
    placed = (
        P(both, None), P(both), P(both, None), P(both), P(both), P(both), P(both, None, None), P(), P(), P(),
    )
    return jax.shard_map(
        body, mesh=mesh, in_specs=placed, out_specs=(P(both, None), P(both, None)), check_vma=False
    )
```

```python
import functools

import jax
import jax.numpy as jnp
from jax import lax
from jax.experimental import pallas as pl
from jax.experimental.pallas import tpu as pltpu
from jax.sharding import PartitionSpec as P

K_DEV = 8
MESH = pl.DeviceIdType.MESH
F32 = jnp.float32
I32 = jnp.int32
BF16 = jnp.bfloat16
LAST = (((1,), (1,)), ((), ()))
PLAIN = (((1,), (0,)), ((), ()))
BACK = PLAIN
EPS = 1e-6


def mm(a, b, dims):
    return lax.dot_general(a, b, dims, preferred_element_type=F32)


def stacked(x, axis):
    hi = x.astype(BF16).astype(F32)
    return jnp.concatenate([hi, x - hi], axis=axis).astype(BF16)


def thirds(x):
    hi = x.astype(BF16).astype(F32)
    mid = (x - hi).astype(BF16).astype(F32)
    return jnp.concatenate([hi, mid, x - hi - mid], axis=0).astype(BF16)


def twice(x):
    both = stacked(x, 0)
    return jnp.concatenate([both, both], axis=1)


def offsets():
    out = []
    for f in range(15):
        if f != 7:
            out.append((f // 5 - 1, f % 5 - 2))
    return out


def kernel(
    groups, blocks, ndir, nblk, entries,
    rhs_hbm, member_hbm, ends_hbm, dir_hbm, reach_hbm, count, sent_hbm, mie_hbm, rot_hbm, trans_hbm,
    coef, factor, rhs, member,
    ends, dirs, reach, sent, mie,
    rot, trans, rot_by, rot_back, tr_by, tr_back, table1, table2, frames, moved, fieldb,
    hc, part, part2, gsum, bsum,
    wsem, send1, recv1, send2, recv2, gs, gr, bs, br,
):
    row = lax.axis_index("grp")
    col = lax.axis_index("blk")
    offs = offsets()
    npeer = len(offs)
    spheres = rhs.shape[0]
    width = 128
    K = K_DEV

    loads = [
        pltpu.make_async_copy(src, dst, wsem.at[i])
        for i, (src, dst) in enumerate([
            (rhs_hbm, rhs), (member_hbm, member), (ends_hbm, ends), (dir_hbm, dirs), (reach_hbm, reach),
            (sent_hbm, sent), (mie_hbm, mie), (rot_hbm, rot), (trans_hbm, trans),
        ])
    ]
    for load in loads:
        load.start()

    partner = 1 - 2 * lax.rem(row, 2)
    other = -partner

    beside = (row + other >= 0) & (row + other < groups)
    near = (-2, 2, -1, 1)

    def valid(dc):
        return ((col + dc >= 0) & (col + dc < blocks)).astype(I32)

    barrier = pltpu.get_barrier_semaphore()
    for j in range(1, groups):
        pl.semaphore_signal(barrier, inc=1, device_id=(lax.rem(row + j, groups), col), device_id_type=MESH)
    for j in range(1, blocks):
        pl.semaphore_signal(barrier, inc=1, device_id=(row, lax.rem(col + j, blocks)), device_id_type=MESH)

    @pl.when(beside)
    def _():
        for dc in near:
            pl.semaphore_signal(barrier, inc=1, device_id=(row + other, col + dc * valid(dc)), device_id_type=MESH)

    cap = sent.shape[0]
    mid = npeer // 2
    for load in loads[:7]:
        load.wait()
    mem = (lax.broadcasted_iota(jnp.int32, (K, spheres), 0) == member[...]).astype(F32)
    agg = mm(jnp.concatenate([mem] * 3, axis=1).astype(BF16), thirds(rhs[...]), PLAIN)
    for g in range(nblk):
        table1[mid, ndir + g] = agg[:, g * width:(g + 1) * width]
    npairs = ends.shape[1]
    live = lax.broadcasted_iota(jnp.int32, (1, npairs), 1) < count[0]
    weight = jnp.where(live, reach[...], 0.0)
    key = dirs[...] * K + ends[0:1, :]
    left = jnp.where(lax.broadcasted_iota(jnp.int32, (ndir * K, npairs), 0) == key, weight, 0.0)
    right = (lax.broadcasted_iota(jnp.int32, (width, npairs), 0) == ends[1:2, :]).astype(F32).astype(BF16)
    own_w = mm(thirds(left), right, LAST)
    own_w = own_w[:ndir * K] + own_w[ndir * K:2 * ndir * K] + own_w[2 * ndir * K:]
    at = lax.broadcasted_iota(jnp.int32, (npeer, width), 1) - (64 + K)
    peer_row = lax.broadcasted_iota(jnp.int32, (npeer, width), 0) * cap
    spread_k = jnp.where((at >= peer_row) & (at < peer_row + cap), 1.0, 0.0)
    wide = mm(sent[...].astype(F32).astype(BF16), spread_k.astype(BF16), PLAIN)
    at4 = lax.broadcasted_iota(jnp.int32, (cap, width), 1) % cap
    row4 = lax.broadcasted_iota(jnp.int32, (cap, width), 0)
    ids = jnp.sum(jnp.where(at4 == (row4 + 64 + K) % cap, wide, 0.0), axis=0, keepdims=True)
    for d in range(ndir):
        tile = own_w[d * K:(d + 1) * K]
        table1[mid, d] = tile + ids if d == 0 else tile

    @pl.when(jnp.logical_not(beside))
    def _():
        empty = pl.ds(5 * (1 - other), 5)
        table1[empty] = jnp.zeros((5,) + table1.shape[1:], F32)
        table2[empty] = jnp.zeros((5,) + table2.shape[1:], F32)

    pl.semaphore_wait(barrier, groups + blocks - 2 + len(near) * beside.astype(I32))

    def copy(table, chunk, i, way, src, dst, send, recv, to_row, to_col):
        tiles = pl.ds(chunk[0], chunk[1] - chunk[0])
        return pltpu.make_async_remote_copy(
            src_ref=table.at[src, tiles], dst_ref=table.at[dst, tiles], send_sem=send.at[i, way], recv_sem=recv.at[i, way],
            device_id=(to_row, to_col), device_id_type=MESH,
        )

    def start_chunk(table, chunk, i, send, recv):
        for dc in near:
            v = valid(dc)
            copy(table, chunk, i, 0, mid, mid + dc * (2 * v - 1), send, recv, row + partner * (1 - v), col + dc * v).start()

        @pl.when(beside)
        def _():
            for dc in near + (0,):
                v = valid(dc)
                at = 5 * (1 + other) + 2 + dc * (2 * v - 1)
                copy(table, chunk, i, 2, mid, at, send, recv, row + other, col + dc * v).start()

    def whole(table, chunk, i, way, send, recv):
        many = pl.ds(0, (len(near), 5, 5)[way])
        return copy(table, chunk, i, way, many, many, send, recv, row + partner, col)

    def wait_send(table, chunk, i, send, recv):
        whole(table, chunk, i, 0, send, recv).wait_send()
        whole(table, chunk, i, 1, send, recv).wait_send()

        @pl.when(beside)
        def _():
            whole(table, chunk, i, 2, send, recv).wait_send()

    def pass_on(table, chunks, i, send, recv):
        whole(table, chunks[i], i, 0, send, recv).wait_recv()
        copy(table, chunks[i], i, 1, pl.ds(5, 5), pl.ds(5 * (1 + partner), 5), send, recv, row + partner, col).start()

    def wait_rest(table, chunks, i, send, recv):
        whole(table, chunks[i], i, 1, send, recv).wait_recv()

        @pl.when(beside)
        def _():
            whole(table, chunks[i], i, 2, send, recv).wait_recv()

    cuts = [0] + [nblk * c // 15 for c in (7,)] + [nblk]
    parts = len(cuts) - 1
    first_blocks = [list(range(a, b)) for a, b in zip(cuts, cuts[1:])]
    second_blocks = [list(range(max(a - 1, 1), b - 1)) for a, b in zip(cuts, cuts[1:])]
    second_blocks[-1] += [nblk - 1, 0]

    def spans(groups_of, lead):
        out, pos = [], 0
        for blocks_of in groups_of:
            end = pos + len(blocks_of) + (lead if not out else 0)
            out.append((pos, end))
            pos = end
        return out

    chunks1, chunks2 = spans(first_blocks, ndir), spans(second_blocks, 0)
    at1 = {g: g + ndir for g in range(nblk)}
    at2 = {g: (g - 1) % nblk for g in range(nblk)}
    plan1 = [[[(0, 0, 0), (0, 0, 1), (1, 0, 0)], [], []], [[(1, 0, 1)], [], []]]
    plan2 = [[[(2, 0, 0), (0, 1, 0), (0, 1, 1), (1, 1, 0)], [], []], [[(3, 0, 0), (3, 0, 1), (3, 1, 0), (3, 1, 1), (1, 1, 1)], [], []]]

    def run(step):
        act, which, j = step
        table, chunks, send, recv = ((table1, chunks1, send1, recv1), (table2, chunks2, send2, recv2))[which]
        if act == 0:
            pass_on(table, chunks, j, send, recv)
        elif act == 1:
            wait_rest(table, chunks, j, send, recv)
        elif act == 2:
            second_line()
        else:
            wait_send(table, chunks[j], j, send, recv)

    for i, chunk in enumerate(chunks1):
        start_chunk(table1, chunk, i, send1, recv1)

    squares = jnp.zeros((K, width), F32)
    for g in range(nblk):
        for s in range(0, spheres, K):
            v = rhs[s:s + K, g * width:(g + 1) * width]
            squares = squares + v * v
    counts = jnp.sum(mem, axis=1, keepdims=True)
    for load in loads[7:]:
        load.wait()
    for g in range(nblk):
        for d in range(ndir):
            rot_by[d, g] = stacked(rot[d, g], 0)
            rot_back[d, g] = stacked(rot[d, g].T, 0)
        tr_by[g] = stacked(trans[g], 0)
        tr_back[g] = stacked(trans[g].T, 0)
    for step in plan1[0][0]:
        run(step)

    rows = (npeer + 1) * K
    lane = lax.broadcasted_iota(jnp.int32, (width, width), 1)
    sub = lax.broadcasted_iota(jnp.int32, (width, width), 0)
    slot = sub // K
    from_row, from_col = row + 1 - slot // 5, col + 2 - slot % 5
    there = (slot <= npeer) & (from_row >= 0) & (from_row < groups) & (from_col >= 0) & (from_col < blocks)
    peer = jnp.where(slot > mid, slot - 1, slot)
    lane8 = lax.broadcasted_iota(jnp.int32, (K, width), 1)
    far = jnp.zeros((K, width), F32)
    for k in range(npeer):
        first = 64 + K + cap * k
        far = far + jnp.where((lane8 >= first) & (lane8 < first + cap), table1[k + (k >= mid), 0], 0.0)
    far = pltpu.roll(far, 64, 1)
    far = jnp.broadcast_to(far[0:1], (width, width))
    low = K + cap * peer
    subk = (sub % K)
    wanted = jnp.where(lane < K, subk.astype(F32), far)
    lane_key = jnp.where(lane < K, lane.astype(F32), subk.astype(F32))
    begin = jnp.where(slot == mid, 0, low)
    end = jnp.where(slot == mid, K, low + cap)
    pick = jnp.where(there & (lane >= begin) & (lane < end) & (wanted == lane_key), 1.0, 0.0).astype(BF16)
    mine = pltpu.roll(jnp.broadcast_to(ids, (K, width)), 64, 1)
    sub8 = lax.broadcasted_iota(jnp.int32, (K, width), 0)
    named = jnp.where(lane8 < K, lane8.astype(F32), mine)
    take = jnp.where((lane8 < 64) & (named == sub8.astype(F32)), 1.0, 0.0).astype(BF16)
    back = K + cap * (npeer - 1 - peer)
    start = jnp.where(slot == mid, 0, back)
    stop = jnp.where(slot == mid, K, back + cap)
    keep = there & (lane >= start) & (lane < stop)
    front_w, behind_w = [], []
    pad = jnp.zeros((width - rows, width), F32)
    for d in range(ndir):
        owned = jnp.where(lane8 < 64, table1[mid, d], 0.0)
        picked = mm(thirds(owned), pick, LAST)
        front_w.append(picked[:K] + picked[K:2 * K] + picked[2 * K:])
        every = jnp.where(keep, jnp.concatenate([table1[:, d].reshape(rows, width), pad], axis=0), 0.0)
        taken = mm(take, thirds(every), LAST)
        behind_w.append(taken[:, :width] + taken[:, width:2 * width] + taken[:, 2 * width:])
    wts = jnp.concatenate(front_w + behind_w, axis=0)
    n_all = wts.shape[0]
    w_both = twice(wts)

    lanes = lax.broadcasted_iota(jnp.int32, (ndir * K, width), 1)
    lanes2 = lax.broadcasted_iota(jnp.int32, (2 * ndir * K, width), 1)
    nd = ndir * K

    def products(jobs):
        both = [twice(x) for x, _, _ in jobs]
        tops = [mm(b, w, dims) for b, (_, w, dims) in zip(both, jobs)]
        return [t[:t.shape[0] // 2] + t[t.shape[0] // 2:] for t in tops]

    def frame_steps(table, place, gs):
        tabs = [stacked(jnp.concatenate([table[:, place[g]].reshape(rows, width), pad], axis=0), 0) for g in gs]
        tops = [mm(w_both, t, PLAIN) for t in tabs]
        jobs = []
        for g, top in zip(gs, tops):
            mix = top[:n_all] + top[n_all:]
            for d in range(ndir):
                x = jnp.concatenate([mix[d * K:(d + 1) * K], mix[nd + d * K:nd + (d + 1) * K]], axis=0)
                jobs.append((x, rot_by[d, g], PLAIN))
        ys = products(jobs)
        for i, g in enumerate(gs):
            y = ys[i * ndir:(i + 1) * ndir]
            frames[g] = pltpu.roll(jnp.concatenate([t[:K] for t in y] + [t[K:] for t in y], axis=0), 64, 1)

    def move_steps(gs):
        jobs = []
        for g in gs:
            x = jnp.where(lanes2 < 64, frames[(g - 1) % nblk], frames[g])
            jobs.append((x[:nd], tr_by[g], PLAIN))
            jobs.append((x[nd:], tr_back[g], BACK))
        ys = products(jobs)
        for i, g in enumerate(gs):
            moved[g] = pltpu.roll(ys[2 * i] + ys[2 * i + 1], 64, 1)

    def field_steps(gs):
        jobs = []
        for g in gs:
            u = jnp.where(lanes < 64, moved[g], moved[(g + 1) % nblk])
            for d in range(ndir):
                jobs.append((u[d * K:(d + 1) * K], rot_back[d, g], BACK))
        ys = products(jobs)
        for i, g in enumerate(gs):
            acc = ys[i * ndir]
            for d in range(1, ndir):
                acc = acc + ys[i * ndir + d]
            fieldb[g] = acc * mie[g:g + 1, :]

    def field_of(table, place, blocks_in, plan, before, after):
        have_f, have_u, have_h = set(), set(), set()
        for i, new in enumerate(blocks_in):
            before(i)
            frame_steps(table, place, new)
            have_f |= set(new)
            for step in plan[i][1]:
                run(step)
            ready = [g for g in range(nblk) if g not in have_u and g in have_f and (g - 1) % nblk in have_f]
            move_steps(ready)
            have_u |= set(ready)
            for step in plan[i][2]:
                run(step)
            ready = [g for g in range(nblk) if g not in have_h and g in have_u and (g + 1) % nblk in have_u]
            field_steps(ready)
            have_h |= set(ready)
            after(i, have_h)

    def line_start(source, sums, send, recv, axis):
        here, size = (row, groups) if axis == 0 else (col, blocks)
        for j in range(1, size):
            peer = lax.rem(here + j, size)
            pltpu.make_async_remote_copy(
                src_ref=source, dst_ref=sums.at[here], send_sem=send.at[0], recv_sem=recv.at[0],
                device_id=(peer, col) if axis == 0 else (row, peer), device_id_type=MESH,
            ).start()

    def line_all(sums, send, recv):
        many = pl.ds(0, sums.shape[0] - 1)
        return pltpu.make_async_remote_copy(
            src_ref=sums.at[many], dst_ref=sums.at[many], send_sem=send.at[0], recv_sem=recv.at[0],
            device_id=(lax.rem(row + 1, groups), col), device_id_type=MESH,
        )

    def second_line():
        line_all(gsum, gs, gr).wait_recv()
        line_all(gsum, gs, gr).wait_send()
        line = gsum[0]
        for j in range(1, groups):
            line = line + gsum[j]
        part2[...] = line
        bsum[col] = line
        line_start(part2, bsum, bs, br, 1)

    sums_in = [jnp.zeros((K, width), F32), jnp.zeros((K, width), F32)]

    def before1(i):
        if i:
            for step in plan1[i][0]:
                run(step)

    def after1(i, have):
        assert set(second_blocks[i]) <= have
        for g in second_blocks[i]:
            h = fieldb[g]
            hc[g] = h
            scaled = h * counts
            table2[mid, at2[g]] = scaled
            sums_in[0] = sums_in[0] + h * table1[mid, at1[g]]
            sums_in[1] = sums_in[1] + h * scaled
        if i == parts - 1:
            fold = lambda t: jnp.sum(t, axis=0, keepdims=True)
            zero = jnp.zeros((K - 3, width), F32)
            mine_part = jnp.concatenate([fold(squares), fold(sums_in[0]), fold(sums_in[1]), zero], axis=0)
            part[...] = mine_part
            gsum[row] = mine_part
            line_start(part, gsum, gs, gr, 0)
        start_chunk(table2, chunks2[i], i, send2, recv2)

    field_of(table1, at1, first_blocks, plan1, before1, after1)

    def before2(i):
        for step in plan2[i][0]:
            run(step)

    field_of(table2, at2, second_blocks, plan2, before2, lambda i, have: None)

    line_all(bsum, bs, br).wait_recv()
    line_all(bsum, bs, br).wait_send()
    sums = bsum[0]
    for j in range(1, blocks):
        sums = sums + bsum[j]
    sums = jnp.sum(sums, axis=1, keepdims=True)
    s_, a_, b_ = sums[0:1], sums[1:2], sums[2:3]
    shift = entries * EPS
    q = (a_ + shift) / (s_ + shift)
    scale2 = (s_ + shift) / entries
    norm2 = (q * q * s_ - 2.0 * q * a_ + b_) / (entries * scale2) + EPS
    inv = 1.0 / jnp.sqrt(scale2 * norm2)
    for g in range(nblk):
        span = slice(g * width, (g + 1) * width)
        h = hc[g]
        coef[:K, span] = h * inv
        coef[K:, span] = (q * h - fieldb[g]) * inv
    factor[...] = jnp.broadcast_to(q * inv, factor.shape)


def closing(coef, factor, rhs, member, basis, image):
    spheres, full = rhs.shape
    mem = (lax.broadcasted_iota(I32, (K_DEV, spheres), 0) == member[...]).astype(BF16)
    mem3 = jnp.concatenate([mem.astype(F32)] * 3, axis=0).astype(BF16)
    scale = factor[0:1, 0:1]
    dims = (((0,), (0,)), ((), ()))

    def spread(x):
        return mm(mem3, thirds(x), dims)

    out = rhs[...] * scale - spread(coef[:K_DEV, :])
    basis[...] = out
    image[...] = out - spread(coef[K_DEV:, :])


def body(rhs, membership, pair_ends, pair_dir, pair_reach, pair_count, send_idx, rotation, translation, mie):
    groups, blocks = lax.axis_size("grp"), lax.axis_size("blk")
    spheres, full = rhs.shape
    ndir, nblk, width = rotation.shape[:3]
    npeer, cap = send_idx.shape[1:]
    npairs = pair_dir.shape[0]
    K = K_DEV
    vm = pl.BlockSpec(memory_space=pltpu.VMEM)
    hb = pl.BlockSpec(memory_space=pl.ANY)
    V, D = pltpu.VMEM, pltpu.SemaphoreType.DMA
    out = jax.ShapeDtypeStruct(rhs.shape, F32)
    entries = float(groups * blocks * spheres * full)
    parts = pl.pallas_call(
        functools.partial(kernel, groups, blocks, ndir, nblk, entries),
        out_shape=(V((2 * K, full), F32), V((K, width), F32), V(rhs.shape, F32), V((1, spheres), I32)),
        in_specs=[hb] * 5 + [pl.BlockSpec(memory_space=pltpu.SMEM)] + [hb] * 4,
        out_specs=(vm,) * 4,
        scratch_shapes=[
            V((2, npairs), I32), V((1, npairs), I32), V((1, npairs), F32), V((cap, npeer), I32), V((nblk, width), F32),
            V(rotation.shape, F32), V(translation.shape, F32),
            V((ndir, nblk, 2 * width, width), BF16), V((ndir, nblk, 2 * width, width), BF16),
            V((nblk, 2 * width, width), BF16), V((nblk, 2 * width, width), BF16),
            V((npeer + 1, nblk + ndir, K, width), F32), V((npeer + 1, nblk, K, width), F32),
            V((nblk, 2 * ndir * K, width), F32), V((nblk, ndir * K, width), F32), V((nblk, K, width), F32),
            V((nblk, K, width), F32), V((K, width), F32), V((K, width), F32), V((groups, K, width), F32), V((blocks, K, width), F32),
            D((9,)), D((2, 3)), D((2, 3)), D((2, 3)), D((2, 3)),
            D((1,)), D((1,)), D((1,)), D((1,)),
        ],
        compiler_params=pltpu.CompilerParams(
            collective_id=0, has_side_effects=True, vmem_limit_bytes=48 << 20
        ),
    )(*[x if x.size == 1 else pltpu.with_memory_space_constraint(x, pltpu.HBM) for x in (
        rhs, membership[None, :], pair_ends.T, pair_dir[None, :], pair_reach[None, :], pair_count,
        send_idx[0].T, mie.reshape(nblk, width), rotation, translation,
    )])
    return pl.pallas_call(
        closing,
        out_shape=(out, out),
        in_specs=[vm] * 4,
        out_specs=(vm, vm),
        compiler_params=pltpu.CompilerParams(vmem_limit_bytes=8 << 20),
    )(*parts)


def solution(mesh):
    both = ("grp", "blk")
    placed = (
        P(both, None), P(both), P(both, None), P(both), P(both), P(both), P(both, None, None), P(), P(), P(),
    )
    return jax.shard_map(
        body, mesh=mesh, in_specs=placed, out_specs=(P(both, None), P(both, None)), check_vma=False
    )
```

```python
import functools

import jax
import jax.numpy as jnp
from jax import lax
from jax.experimental import pallas as pl
from jax.experimental.pallas import tpu as pltpu
from jax.sharding import PartitionSpec as P

K_DEV = 8
MESH = pl.DeviceIdType.MESH
F32 = jnp.float32
I32 = jnp.int32
BF16 = jnp.bfloat16
LAST = (((1,), (1,)), ((), ()))
PLAIN = (((1,), (0,)), ((), ()))
BACK = PLAIN
EPS = 1e-6


def mm(a, b, dims):
    return lax.dot_general(a, b, dims, preferred_element_type=F32)


def stacked(x, axis):
    hi = x.astype(BF16).astype(F32)
    return jnp.concatenate([hi, x - hi], axis=axis).astype(BF16)


def thirds(x):
    hi = x.astype(BF16).astype(F32)
    mid = (x - hi).astype(BF16).astype(F32)
    return jnp.concatenate([hi, mid, x - hi - mid], axis=0).astype(BF16)


def twice(x):
    both = stacked(x, 0)
    return jnp.concatenate([both, both], axis=1)


def offsets():
    out = []
    for f in range(15):
        if f != 7:
            out.append((f // 5 - 1, f % 5 - 2))
    return out


def kernel(
    groups, blocks, ndir, nblk, entries,
    rhs_hbm, member_hbm, ends_hbm, dir_hbm, reach_hbm, count, sent_hbm, mie_hbm, rot_hbm, trans_hbm,
    coef, factor, rhs, member,
    ends, dirs, reach, sent, mie,
    rot, trans, rot_by, rot_back, tr_by, tr_back, table1, table2, frames, moved, fieldb,
    hc, part, part2, gsum, bsum,
    wsem, send1, recv1, send2, recv2, gs, gr, bs, br,
):
    row = lax.axis_index("grp")
    col = lax.axis_index("blk")
    offs = offsets()
    npeer = len(offs)
    spheres = rhs.shape[0]
    width = 128
    K = K_DEV

    loads = [
        pltpu.make_async_copy(src, dst, wsem.at[i])
        for i, (src, dst) in enumerate([
            (rhs_hbm, rhs), (member_hbm, member), (ends_hbm, ends), (dir_hbm, dirs), (reach_hbm, reach),
            (sent_hbm, sent), (mie_hbm, mie), (rot_hbm, rot), (trans_hbm, trans),
        ])
    ]
    for load in loads[:7]:
        load.start()

    partner = 1 - 2 * lax.rem(row, 2)
    other = -partner

    beside = (row + other >= 0) & (row + other < groups)
    near = (-2, 2, -1, 1)

    def valid(dc):
        return ((col + dc >= 0) & (col + dc < blocks)).astype(I32)

    barrier = pltpu.get_barrier_semaphore()
    for j in range(1, groups):
        pl.semaphore_signal(barrier, inc=1, device_id=(lax.rem(row + j, groups), col), device_id_type=MESH)
    for j in range(1, blocks):
        pl.semaphore_signal(barrier, inc=1, device_id=(row, lax.rem(col + j, blocks)), device_id_type=MESH)

    @pl.when(beside)
    def _():
        for dc in near:
            pl.semaphore_signal(barrier, inc=1, device_id=(row + other, col + dc * valid(dc)), device_id_type=MESH)

    cap = sent.shape[0]
    mid = npeer // 2
    for load in loads[:7]:
        load.wait()
    for load in loads[7:]:
        load.start()
    mem = (lax.broadcasted_iota(jnp.int32, (K, spheres), 0) == member[...]).astype(F32)
    agg = mm(jnp.concatenate([mem] * 3, axis=1).astype(BF16), thirds(rhs[...]), PLAIN)
    lead = ndir // 2 + 1
    for g in range(nblk):
        table1[mid, lead + g] = agg[:, g * width:(g + 1) * width]
    npairs = ends.shape[1]
    live = lax.broadcasted_iota(jnp.int32, (1, npairs), 1) < count[0]
    weight = jnp.where(live, reach[...], 0.0)
    key = dirs[...] * K + ends[0:1, :]
    left = jnp.where(lax.broadcasted_iota(jnp.int32, (ndir * K, npairs), 0) == key, weight, 0.0)
    right = (lax.broadcasted_iota(jnp.int32, (width, npairs), 0) == ends[1:2, :]).astype(F32).astype(BF16)
    own_w = mm(thirds(left), right, LAST)
    own_w = own_w[:ndir * K] + own_w[ndir * K:2 * ndir * K] + own_w[2 * ndir * K:]
    at = lax.broadcasted_iota(jnp.int32, (npeer, width), 1) - (64 + K)
    peer_row = lax.broadcasted_iota(jnp.int32, (npeer, width), 0) * cap
    spread_k = jnp.where((at >= peer_row) & (at < peer_row + cap), 1.0, 0.0)
    wide = mm(sent[...].astype(F32).astype(BF16), spread_k.astype(BF16), PLAIN)
    at4 = lax.broadcasted_iota(jnp.int32, (cap, width), 1) % cap
    row4 = lax.broadcasted_iota(jnp.int32, (cap, width), 0)
    ids = jnp.sum(jnp.where(at4 == (row4 + 64 + K) % cap, wide, 0.0), axis=0, keepdims=True)
    packed = [own_w[d * K:(d + 1) * K] for d in range(ndir)] + [jnp.broadcast_to(ids, (K, width))]
    for t in range(lead):
        second = packed[2 * t + 1]
        table1[mid, t] = packed[2 * t] + (second if 2 * t + 1 == ndir else pltpu.roll(second, 64, 1))

    @pl.when(jnp.logical_not(beside))
    def _():
        empty = pl.ds(5 * (1 - other), 5)
        table1[empty] = jnp.zeros((5,) + table1.shape[1:], F32)
        table2[empty] = jnp.zeros((5,) + table2.shape[1:], F32)

    pl.semaphore_wait(barrier, groups + blocks - 2 + len(near) * beside.astype(I32))

    def copy(table, chunk, i, way, src, dst, send, recv, to_row, to_col):
        tiles = pl.ds(chunk[0], chunk[1] - chunk[0])
        return pltpu.make_async_remote_copy(
            src_ref=table.at[src, tiles], dst_ref=table.at[dst, tiles], send_sem=send.at[i, way], recv_sem=recv.at[i, way],
            device_id=(to_row, to_col), device_id_type=MESH,
        )

    def start_chunk(table, chunk, i, send, recv):
        for dc in near:
            v = valid(dc)
            copy(table, chunk, i, 0, mid, mid + dc * (2 * v - 1), send, recv, row + partner * (1 - v), col + dc * v).start()

        @pl.when(beside)
        def _():
            for dc in near + (0,):
                v = valid(dc)
                at = 5 * (1 + other) + 2 + dc * (2 * v - 1)
                copy(table, chunk, i, 2, mid, at, send, recv, row + other, col + dc * v).start()

    def whole(table, chunk, i, way, send, recv):
        many = pl.ds(0, (len(near), 5, 5)[way])
        return copy(table, chunk, i, way, many, many, send, recv, row + partner, col)

    def wait_send(table, chunk, i, send, recv):
        whole(table, chunk, i, 0, send, recv).wait_send()
        whole(table, chunk, i, 1, send, recv).wait_send()

        @pl.when(beside)
        def _():
            whole(table, chunk, i, 2, send, recv).wait_send()

    def pass_on(table, chunks, i, send, recv):
        whole(table, chunks[i], i, 0, send, recv).wait_recv()
        copy(table, chunks[i], i, 1, pl.ds(5, 5), pl.ds(5 * (1 + partner), 5), send, recv, row + partner, col).start()

    def wait_rest(table, chunks, i, send, recv):
        whole(table, chunks[i], i, 1, send, recv).wait_recv()

        @pl.when(beside)
        def _():
            whole(table, chunks[i], i, 2, send, recv).wait_recv()

    cuts = [0] + [nblk * c // 15 for c in (8,)] + [nblk]
    parts = len(cuts) - 1
    first_blocks = [list(range(a, b)) for a, b in zip(cuts, cuts[1:])]
    second_blocks = [list(range(max(a - 1, 1), b - 1)) for a, b in zip(cuts, cuts[1:])]
    second_blocks[-1] += [nblk - 1, 0]

    def spans(groups_of, lead):
        out, pos = [], 0
        for blocks_of in groups_of:
            end = pos + len(blocks_of) + (lead if not out else 0)
            out.append((pos, end))
            pos = end
        return out

    chunks1, chunks2 = spans(first_blocks, lead), spans(second_blocks, 0)
    at1 = {g: g + lead for g in range(nblk)}
    at2 = {g: (g - 1) % nblk for g in range(nblk)}
    plan1 = [[[(0, 0, 0), (0, 0, 1), (1, 0, 0)], [], []], [[(1, 0, 1)], [], []]]
    plan2 = [[[(2, 0, 0), (0, 1, 0), (0, 1, 1), (1, 1, 0)], [], []], [[(3, 0, 0), (3, 0, 1), (3, 1, 0), (3, 1, 1), (1, 1, 1)], [], []]]

    def run(step):
        act, which, j = step
        table, chunks, send, recv = ((table1, chunks1, send1, recv1), (table2, chunks2, send2, recv2))[which]
        if act == 0:
            pass_on(table, chunks, j, send, recv)
        elif act == 1:
            wait_rest(table, chunks, j, send, recv)
        elif act == 2:
            second_line()
        else:
            wait_send(table, chunks[j], j, send, recv)

    for i, chunk in enumerate(chunks1):
        start_chunk(table1, chunk, i, send1, recv1)

    squares = jnp.zeros((K, width), F32)
    for g in range(nblk):
        for s in range(0, spheres, K):
            v = rhs[s:s + K, g * width:(g + 1) * width]
            squares = squares + v * v
    counts = jnp.sum(mem, axis=1, keepdims=True)
    for load in loads[7:]:
        load.wait()
    for g in range(nblk):
        for d in range(ndir):
            rot_by[d, g] = stacked(rot[d, g], 0)
            rot_back[d, g] = stacked(rot[d, g].T, 0)
        tr_by[g] = stacked(trans[g], 0)
        tr_back[g] = stacked(trans[g].T, 0)
    for step in plan1[0][0]:
        run(step)

    rows = (npeer + 1) * K
    lane = lax.broadcasted_iota(jnp.int32, (width, width), 1)
    sub = lax.broadcasted_iota(jnp.int32, (width, width), 0)
    slot = sub // K
    from_row, from_col = row + 1 - slot // 5, col + 2 - slot % 5
    there = (slot <= npeer) & (from_row >= 0) & (from_row < groups) & (from_col >= 0) & (from_col < blocks)
    peer = jnp.where(slot > mid, slot - 1, slot)
    lane8 = lax.broadcasted_iota(jnp.int32, (K, width), 1)
    far = jnp.zeros((K, width), F32)
    for k in range(npeer):
        first = 64 + K + cap * k
        far = far + jnp.where((lane8 >= first) & (lane8 < first + cap), table1[k + (k >= mid), lead - 1], 0.0)
    far = pltpu.roll(far, 64, 1)
    far = jnp.broadcast_to(far[0:1], (width, width))
    low = K + cap * peer
    subk = (sub % K)
    wanted = jnp.where(lane < K, subk.astype(F32), far)
    lane_key = jnp.where(lane < K, lane.astype(F32), subk.astype(F32))
    begin = jnp.where(slot == mid, 0, low)
    end = jnp.where(slot == mid, K, low + cap)
    pick = jnp.where(there & (lane >= begin) & (lane < end) & (wanted == lane_key), 1.0, 0.0).astype(BF16)
    mine = pltpu.roll(jnp.broadcast_to(ids, (K, width)), 64, 1)
    sub8 = lax.broadcasted_iota(jnp.int32, (K, width), 0)
    named = jnp.where(lane8 < K, lane8.astype(F32), mine)
    take = jnp.where((lane8 < 64) & (named == sub8.astype(F32)), 1.0, 0.0).astype(BF16)
    back = K + cap * (npeer - 1 - peer)
    start = jnp.where(slot == mid, 0, back)
    stop = jnp.where(slot == mid, K, back + cap)
    keep = there & (lane >= start) & (lane < stop)
    front_w, behind_w = [], []
    pad = jnp.zeros((width - rows, width), F32)
    for d in range(ndir):
        halved = lambda t: pltpu.roll(t, 64, 1) if d % 2 else t
        owned = jnp.where(lane8 < 64, halved(table1[mid, d // 2]), 0.0)
        picked = mm(thirds(owned), pick, LAST)
        front_w.append(picked[:K] + picked[K:2 * K] + picked[2 * K:])
        every = jnp.where(keep, halved(jnp.concatenate([table1[:, d // 2].reshape(rows, width), pad], axis=0)), 0.0)
        taken = mm(take, thirds(every), LAST)
        behind_w.append(taken[:, :width] + taken[:, width:2 * width] + taken[:, 2 * width:])
    wts = jnp.concatenate(front_w + behind_w, axis=0)
    n_all = wts.shape[0]
    w_both = twice(wts)

    lanes = lax.broadcasted_iota(jnp.int32, (ndir * K, width), 1)
    lanes2 = lax.broadcasted_iota(jnp.int32, (2 * ndir * K, width), 1)
    nd = ndir * K

    def products(jobs):
        both = [twice(x) for x, _, _ in jobs]
        tops = [mm(b, w, dims) for b, (_, w, dims) in zip(both, jobs)]
        return [t[:t.shape[0] // 2] + t[t.shape[0] // 2:] for t in tops]

    def frame_steps(table, place, gs):
        tabs = [stacked(jnp.concatenate([table[:, place[g]].reshape(rows, width), pad], axis=0), 0) for g in gs]
        pairs = [mm(w_both, jnp.concatenate(tabs[i:i + 2], axis=1), PLAIN) for i in range(0, len(gs), 2)]
        tops = [pairs[i // 2][:, i % 2 * width:(i % 2 + 1) * width] for i in range(len(gs))]
        jobs = []
        for g, top in zip(gs, tops):
            mix = top[:n_all] + top[n_all:]
            for d in range(ndir):
                x = jnp.concatenate([mix[d * K:(d + 1) * K], mix[nd + d * K:nd + (d + 1) * K]], axis=0)
                jobs.append((x, rot_by[d, g], PLAIN))
        ys = products(jobs)
        for i, g in enumerate(gs):
            y = ys[i * ndir:(i + 1) * ndir]
            frames[g] = pltpu.roll(jnp.concatenate([t[:K] for t in y] + [t[K:] for t in y], axis=0), 64, 1)

    def move_steps(gs):
        jobs = []
        for g in gs:
            x = jnp.where(lanes2 < 64, frames[(g - 1) % nblk], frames[g])
            jobs.append((x[:nd], tr_by[g], PLAIN))
            jobs.append((x[nd:], tr_back[g], BACK))
        ys = products(jobs)
        for i, g in enumerate(gs):
            moved[g] = pltpu.roll(ys[2 * i] + ys[2 * i + 1], 64, 1)

    def field_steps(gs):
        jobs = []
        for g in gs:
            u = jnp.where(lanes < 64, moved[g], moved[(g + 1) % nblk])
            for d in range(ndir):
                jobs.append((u[d * K:(d + 1) * K], rot_back[d, g], BACK))
        ys = products(jobs)
        for i, g in enumerate(gs):
            acc = ys[i * ndir]
            for d in range(1, ndir):
                acc = acc + ys[i * ndir + d]
            fieldb[g] = acc * mie[g:g + 1, :]

    def field_of(table, place, blocks_in, plan, before, after):
        have_f, have_u, have_h = set(), set(), set()
        for i, new in enumerate(blocks_in):
            before(i)
            frame_steps(table, place, new)
            have_f |= set(new)
            for step in plan[i][1]:
                run(step)
            ready = [g for g in range(nblk) if g not in have_u and g in have_f and (g - 1) % nblk in have_f]
            move_steps(ready)
            have_u |= set(ready)
            for step in plan[i][2]:
                run(step)
            ready = [g for g in range(nblk) if g not in have_h and g in have_u and (g + 1) % nblk in have_u]
            field_steps(ready)
            have_h |= set(ready)
            after(i, have_h)

    def line_start(source, sums, send, recv, axis):
        here, size = (row, groups) if axis == 0 else (col, blocks)
        for j in range(1, size):
            peer = lax.rem(here + j, size)
            pltpu.make_async_remote_copy(
                src_ref=source, dst_ref=sums.at[here], send_sem=send.at[0], recv_sem=recv.at[0],
                device_id=(peer, col) if axis == 0 else (row, peer), device_id_type=MESH,
            ).start()

    def line_all(sums, send, recv):
        many = pl.ds(0, sums.shape[0] - 1)
        return pltpu.make_async_remote_copy(
            src_ref=sums.at[many], dst_ref=sums.at[many], send_sem=send.at[0], recv_sem=recv.at[0],
            device_id=(lax.rem(row + 1, groups), col), device_id_type=MESH,
        )

    def second_line():
        line_all(gsum, gs, gr).wait_recv()
        line_all(gsum, gs, gr).wait_send()
        line = gsum[0]
        for j in range(1, groups):
            line = line + gsum[j]
        part2[...] = line
        bsum[col] = line
        line_start(part2, bsum, bs, br, 1)

    sums_in = [jnp.zeros((K, width), F32), jnp.zeros((K, width), F32)]

    def before1(i):
        if i:
            for step in plan1[i][0]:
                run(step)

    def after1(i, have):
        assert set(second_blocks[i]) <= have
        for g in second_blocks[i]:
            h = fieldb[g]
            hc[g] = h
            scaled = h * counts
            table2[mid, at2[g]] = scaled
            sums_in[0] = sums_in[0] + h * table1[mid, at1[g]]
            sums_in[1] = sums_in[1] + h * scaled
        if i == parts - 1:
            fold = lambda t: jnp.sum(t, axis=0, keepdims=True)
            zero = jnp.zeros((K - 3, width), F32)
            mine_part = jnp.concatenate([fold(squares), fold(sums_in[0]), fold(sums_in[1]), zero], axis=0)
            part[...] = mine_part
            gsum[row] = mine_part
            line_start(part, gsum, gs, gr, 0)
        start_chunk(table2, chunks2[i], i, send2, recv2)

    field_of(table1, at1, first_blocks, plan1, before1, after1)

    def before2(i):
        for step in plan2[i][0]:
            run(step)

    field_of(table2, at2, second_blocks, plan2, before2, lambda i, have: None)

    line_all(bsum, bs, br).wait_recv()
    line_all(bsum, bs, br).wait_send()
    sums = bsum[0]
    for j in range(1, blocks):
        sums = sums + bsum[j]
    sums = jnp.sum(sums, axis=1, keepdims=True)
    s_, a_, b_ = sums[0:1], sums[1:2], sums[2:3]
    shift = entries * EPS
    q = (a_ + shift) / (s_ + shift)
    scale2 = (s_ + shift) / entries
    norm2 = (q * q * s_ - 2.0 * q * a_ + b_) / (entries * scale2) + EPS
    inv = 1.0 / jnp.sqrt(scale2 * norm2)
    for g in range(nblk):
        span = slice(g * width, (g + 1) * width)
        h = hc[g]
        coef[:K, span] = h * inv
        coef[K:, span] = (q * h - fieldb[g]) * inv
    factor[...] = jnp.broadcast_to(q * inv, factor.shape)


def closing(coef, factor, rhs, member, basis, image):
    spheres, full = rhs.shape
    mem = (lax.broadcasted_iota(I32, (K_DEV, spheres), 0) == member[...]).astype(BF16)
    mem3 = jnp.concatenate([mem.astype(F32)] * 3, axis=0).astype(BF16)
    scale = factor[0:1, 0:1]
    dims = (((0,), (0,)), ((), ()))

    def spread(x):
        return mm(mem3, thirds(x), dims)

    out = rhs[...] * scale - spread(coef[:K_DEV, :])
    basis[...] = out
    image[...] = out - spread(coef[K_DEV:, :])


def body(rhs, membership, pair_ends, pair_dir, pair_reach, pair_count, send_idx, rotation, translation, mie):
    groups, blocks = lax.axis_size("grp"), lax.axis_size("blk")
    spheres, full = rhs.shape
    ndir, nblk, width = rotation.shape[:3]
    npeer, cap = send_idx.shape[1:]
    npairs = pair_dir.shape[0]
    K = K_DEV
    vm = pl.BlockSpec(memory_space=pltpu.VMEM)
    hb = pl.BlockSpec(memory_space=pl.ANY)
    V, D = pltpu.VMEM, pltpu.SemaphoreType.DMA
    out = jax.ShapeDtypeStruct(rhs.shape, F32)
    entries = float(groups * blocks * spheres * full)
    parts = pl.pallas_call(
        functools.partial(kernel, groups, blocks, ndir, nblk, entries),
        out_shape=(V((2 * K, full), F32), V((K, width), F32), V(rhs.shape, F32), V((1, spheres), I32)),
        in_specs=[hb] * 5 + [pl.BlockSpec(memory_space=pltpu.SMEM)] + [hb] * 4,
        out_specs=(vm,) * 4,
        scratch_shapes=[
            V((2, npairs), I32), V((1, npairs), I32), V((1, npairs), F32), V((cap, npeer), I32), V((nblk, width), F32),
            V(rotation.shape, F32), V(translation.shape, F32),
            V((ndir, nblk, 2 * width, width), BF16), V((ndir, nblk, 2 * width, width), BF16),
            V((nblk, 2 * width, width), BF16), V((nblk, 2 * width, width), BF16),
            V((npeer + 1, nblk + ndir // 2 + 1, K, width), F32), V((npeer + 1, nblk, K, width), F32),
            V((nblk, 2 * ndir * K, width), F32), V((nblk, ndir * K, width), F32), V((nblk, K, width), F32),
            V((nblk, K, width), F32), V((K, width), F32), V((K, width), F32), V((groups, K, width), F32), V((blocks, K, width), F32),
            D((9,)), D((2, 3)), D((2, 3)), D((2, 3)), D((2, 3)),
            D((1,)), D((1,)), D((1,)), D((1,)),
        ],
        compiler_params=pltpu.CompilerParams(
            collective_id=0, has_side_effects=True, vmem_limit_bytes=48 << 20
        ),
    )(*[x if x.size == 1 else pltpu.with_memory_space_constraint(x, pltpu.HBM) for x in (
        rhs, membership[None, :], pair_ends.T, pair_dir[None, :], pair_reach[None, :], pair_count,
        send_idx[0].T, mie.reshape(nblk, width), rotation, translation,
    )])
    return pl.pallas_call(
        closing,
        out_shape=(out, out),
        in_specs=[vm] * 4,
        out_specs=(vm, vm),
        compiler_params=pltpu.CompilerParams(vmem_limit_bytes=8 << 20),
    )(*parts)


def solution(mesh):
    both = ("grp", "blk")
    placed = (
        P(both, None), P(both), P(both, None), P(both), P(both), P(both), P(both, None, None), P(), P(), P(),
    )
    return jax.shard_map(
        body, mesh=mesh, in_specs=placed, out_specs=(P(both, None), P(both, None)), check_vma=False
    )
```

```python
import functools

import jax
import jax.numpy as jnp
from jax import lax
from jax.experimental import pallas as pl
from jax.experimental.pallas import tpu as pltpu
from jax.sharding import PartitionSpec as P

K_DEV = 8
MESH = pl.DeviceIdType.MESH
F32 = jnp.float32
I32 = jnp.int32
BF16 = jnp.bfloat16
LAST = (((1,), (1,)), ((), ()))
PLAIN = (((1,), (0,)), ((), ()))
BACK = PLAIN
EPS = 1e-6


def mm(a, b, dims):
    return lax.dot_general(a, b, dims, preferred_element_type=F32)


def stacked(x, axis):
    hi = x.astype(BF16).astype(F32)
    return jnp.concatenate([hi, x - hi], axis=axis).astype(BF16)


def thirds(x):
    hi = x.astype(BF16).astype(F32)
    mid = (x - hi).astype(BF16).astype(F32)
    return jnp.concatenate([hi, mid, x - hi - mid], axis=0).astype(BF16)


def twice(x):
    both = stacked(x, 0)
    return jnp.concatenate([both, both], axis=1)


def offsets():
    out = []
    for f in range(15):
        if f != 7:
            out.append((f // 5 - 1, f % 5 - 2))
    return out


def kernel(
    groups, blocks, ndir, nblk, entries,
    rhs_hbm, member_hbm, ends_hbm, dir_hbm, reach_hbm, count, sent_hbm, mie_hbm, rot_hbm, trans_hbm,
    coef, factor, rhs, member,
    ends, dirs, reach, sent, mie,
    rot, trans, rot_by, rot_back, tr_by, tr_back, table1, table2, frames, moved, fieldb,
    hc, part, part2, gsum, bsum,
    wsem, send1, recv1, send2, recv2, gs, gr, bs, br,
):
    row = lax.axis_index("grp")
    col = lax.axis_index("blk")
    offs = offsets()
    npeer = len(offs)
    spheres = rhs.shape[0]
    width = 128
    K = K_DEV

    loads = [
        pltpu.make_async_copy(src, dst, wsem.at[i])
        for i, (src, dst) in enumerate([
            (rhs_hbm, rhs), (member_hbm, member), (ends_hbm, ends), (dir_hbm, dirs), (reach_hbm, reach),
            (sent_hbm, sent), (mie_hbm, mie), (rot_hbm, rot), (trans_hbm, trans),
        ])
    ]
    for load in loads[:7]:
        load.start()

    partner = 1 - 2 * lax.rem(row, 2)
    other = -partner

    beside = (row + other >= 0) & (row + other < groups)
    near = (-2, 2, -1, 1)

    def valid(dc):
        return ((col + dc >= 0) & (col + dc < blocks)).astype(I32)

    barrier = pltpu.get_barrier_semaphore()
    distance = max(2, blocks - 1 - 4)
    for j in range(1, groups):
        pl.semaphore_signal(barrier, inc=1, device_id=(lax.rem(row + j, groups), col), device_id_type=MESH)
    for dc in [d for d in range(-distance, distance + 1) if d]:
        v = valid(dc)
        pl.semaphore_signal(barrier, inc=1, device_id=(row + partner * (1 - v), col + dc * v), device_id_type=MESH)

    @pl.when(beside)
    def _():
        for dc in near:
            pl.semaphore_signal(barrier, inc=1, device_id=(row + other, col + dc * valid(dc)), device_id_type=MESH)

    cap = sent.shape[0]
    mid = npeer // 2
    for load in loads[:7]:
        load.wait()
    for load in loads[7:]:
        load.start()
    mem = (lax.broadcasted_iota(jnp.int32, (K, spheres), 0) == member[...]).astype(F32)
    agg = mm(jnp.concatenate([mem] * 3, axis=1).astype(BF16), thirds(rhs[...]), PLAIN)
    lead = ndir // 2 + 1
    for g in range(nblk):
        table1[mid, lead + g] = agg[:, g * width:(g + 1) * width]
    npairs = ends.shape[1]
    live = lax.broadcasted_iota(jnp.int32, (1, npairs), 1) < count[0]
    weight = jnp.where(live, reach[...], 0.0)
    key = dirs[...] * K + ends[0:1, :]
    left = jnp.where(lax.broadcasted_iota(jnp.int32, (ndir * K, npairs), 0) == key, weight, 0.0)
    right = (lax.broadcasted_iota(jnp.int32, (width, npairs), 0) == ends[1:2, :]).astype(F32).astype(BF16)
    own_w = mm(thirds(left), right, LAST)
    own_w = own_w[:ndir * K] + own_w[ndir * K:2 * ndir * K] + own_w[2 * ndir * K:]
    at = lax.broadcasted_iota(jnp.int32, (npeer, width), 1) - (64 + K)
    peer_row = lax.broadcasted_iota(jnp.int32, (npeer, width), 0) * cap
    spread_k = jnp.where((at >= peer_row) & (at < peer_row + cap), 1.0, 0.0)
    wide = mm(sent[...].astype(F32).astype(BF16), spread_k.astype(BF16), PLAIN)
    at4 = lax.broadcasted_iota(jnp.int32, (cap, width), 1) % cap
    row4 = lax.broadcasted_iota(jnp.int32, (cap, width), 0)
    ids = jnp.sum(jnp.where(at4 == (row4 + 64 + K) % cap, wide, 0.0), axis=0, keepdims=True)
    packed = [own_w[d * K:(d + 1) * K] for d in range(ndir)] + [jnp.broadcast_to(ids, (K, width))]
    for t in range(lead):
        second = packed[2 * t + 1]
        table1[mid, t] = packed[2 * t] + (second if 2 * t + 1 == ndir else pltpu.roll(second, 64, 1))

    @pl.when(jnp.logical_not(beside))
    def _():
        empty = pl.ds(5 * (1 - other), 5)
        table1[empty] = jnp.zeros((5,) + table1.shape[1:], F32)
        table2[empty] = jnp.zeros((5,) + table2.shape[1:], F32)

    pl.semaphore_wait(barrier, groups - 1 + 2 * distance + len(near) * beside.astype(I32))

    def copy(table, chunk, i, way, src, dst, send, recv, to_row, to_col):
        tiles = pl.ds(chunk[0], chunk[1] - chunk[0])
        return pltpu.make_async_remote_copy(
            src_ref=table.at[src, tiles], dst_ref=table.at[dst, tiles], send_sem=send.at[i, way], recv_sem=recv.at[i, way],
            device_id=(to_row, to_col), device_id_type=MESH,
        )

    def start_chunk(table, chunk, i, send, recv):
        for dc in near:
            v = valid(dc)
            copy(table, chunk, i, 0, mid, mid + dc * (2 * v - 1), send, recv, row + partner * (1 - v), col + dc * v).start()

        @pl.when(beside)
        def _():
            for dc in near + (0,):
                v = valid(dc)
                at = 5 * (1 + other) + 2 + dc * (2 * v - 1)
                copy(table, chunk, i, 2, mid, at, send, recv, row + other, col + dc * v).start()

    def whole(table, chunk, i, way, send, recv):
        many = pl.ds(0, (len(near), 5, 5)[way])
        return copy(table, chunk, i, way, many, many, send, recv, row + partner, col)

    def wait_send(table, chunk, i, send, recv):
        whole(table, chunk, i, 0, send, recv).wait_send()
        whole(table, chunk, i, 1, send, recv).wait_send()

        @pl.when(beside)
        def _():
            whole(table, chunk, i, 2, send, recv).wait_send()

    def pass_on(table, chunks, i, send, recv):
        whole(table, chunks[i], i, 0, send, recv).wait_recv()
        copy(table, chunks[i], i, 1, pl.ds(5, 5), pl.ds(5 * (1 + partner), 5), send, recv, row + partner, col).start()

    def wait_rest(table, chunks, i, send, recv):
        whole(table, chunks[i], i, 1, send, recv).wait_recv()

        @pl.when(beside)
        def _():
            whole(table, chunks[i], i, 2, send, recv).wait_recv()

    cuts = [0] + [nblk * c // 15 for c in (8,)] + [nblk]
    parts = len(cuts) - 1
    first_blocks = [list(range(a, b)) for a, b in zip(cuts, cuts[1:])]
    second_blocks = [list(range(max(a - 1, 1), b - 1)) for a, b in zip(cuts, cuts[1:])]
    second_blocks[-1] += [nblk - 1, 0]

    def spans(groups_of, lead):
        out, pos = [], 0
        for blocks_of in groups_of:
            end = pos + len(blocks_of) + (lead if not out else 0)
            out.append((pos, end))
            pos = end
        return out

    chunks1, chunks2 = spans(first_blocks, lead), spans(second_blocks, 0)
    at1 = {g: g + lead for g in range(nblk)}
    at2 = {g: (g - 1) % nblk for g in range(nblk)}
    plan1 = [[[(0, 0, 0), (0, 0, 1), (1, 0, 0)], [], []], [[(1, 0, 1)], [], []]]
    plan2 = [[[(0, 1, 0), (2, 0, 0), (0, 1, 1), (1, 1, 0)], [], []], [[(3, 0, 0), (3, 0, 1), (3, 1, 0), (3, 1, 1), (1, 1, 1)], [], []]]

    def run(step):
        act, which, j = step
        table, chunks, send, recv = ((table1, chunks1, send1, recv1), (table2, chunks2, send2, recv2))[which]
        if act == 0:
            pass_on(table, chunks, j, send, recv)
        elif act == 1:
            wait_rest(table, chunks, j, send, recv)
        elif act == 2:
            second_line()
        else:
            wait_send(table, chunks[j], j, send, recv)

    for i, chunk in enumerate(chunks1):
        start_chunk(table1, chunk, i, send1, recv1)

    squares = jnp.zeros((K, width), F32)
    for g in range(nblk):
        for s in range(0, spheres, K):
            v = rhs[s:s + K, g * width:(g + 1) * width]
            squares = squares + v * v
    counts = jnp.sum(mem, axis=1, keepdims=True)
    for load in loads[7:]:
        load.wait()
    for g in range(nblk):
        for d in range(ndir):
            rot_by[d, g] = stacked(rot[d, g], 0)
            rot_back[d, g] = stacked(rot[d, g].T, 0)
        tr_by[g] = stacked(trans[g], 0)
        tr_back[g] = stacked(trans[g].T, 0)
    for step in plan1[0][0]:
        run(step)

    rows = (npeer + 1) * K
    lane = lax.broadcasted_iota(jnp.int32, (width, width), 1)
    sub = lax.broadcasted_iota(jnp.int32, (width, width), 0)
    slot = sub // K
    from_row, from_col = row + 1 - slot // 5, col + 2 - slot % 5
    there = (slot <= npeer) & (from_row >= 0) & (from_row < groups) & (from_col >= 0) & (from_col < blocks)
    peer = jnp.where(slot > mid, slot - 1, slot)
    lane8 = lax.broadcasted_iota(jnp.int32, (K, width), 1)
    far = jnp.zeros((K, width), F32)
    for k in range(npeer):
        first = 64 + K + cap * k
        far = far + jnp.where((lane8 >= first) & (lane8 < first + cap), table1[k + (k >= mid), lead - 1], 0.0)
    far = pltpu.roll(far, 64, 1)
    far = jnp.broadcast_to(far[0:1], (width, width))
    low = K + cap * peer
    subk = (sub % K)
    wanted = jnp.where(lane < K, subk.astype(F32), far)
    lane_key = jnp.where(lane < K, lane.astype(F32), subk.astype(F32))
    begin = jnp.where(slot == mid, 0, low)
    end = jnp.where(slot == mid, K, low + cap)
    pick = jnp.where(there & (lane >= begin) & (lane < end) & (wanted == lane_key), 1.0, 0.0).astype(BF16)
    mine = pltpu.roll(jnp.broadcast_to(ids, (K, width)), 64, 1)
    sub8 = lax.broadcasted_iota(jnp.int32, (K, width), 0)
    named = jnp.where(lane8 < K, lane8.astype(F32), mine)
    take = jnp.where((lane8 < 64) & (named == sub8.astype(F32)), 1.0, 0.0).astype(BF16)
    back = K + cap * (npeer - 1 - peer)
    start = jnp.where(slot == mid, 0, back)
    stop = jnp.where(slot == mid, K, back + cap)
    keep = there & (lane >= start) & (lane < stop)
    front_w, behind_w = [], []
    pad = jnp.zeros((width - rows, width), F32)
    for d in range(ndir):
        halved = lambda t: pltpu.roll(t, 64, 1) if d % 2 else t
        owned = jnp.where(lane8 < 64, halved(table1[mid, d // 2]), 0.0)
        picked = mm(thirds(owned), pick, LAST)
        front_w.append(picked[:K] + picked[K:2 * K] + picked[2 * K:])
        every = jnp.where(keep, halved(jnp.concatenate([table1[:, d // 2].reshape(rows, width), pad], axis=0)), 0.0)
        taken = mm(take, thirds(every), LAST)
        behind_w.append(taken[:, :width] + taken[:, width:2 * width] + taken[:, 2 * width:])
    wts = jnp.concatenate(front_w + behind_w, axis=0)
    n_all = wts.shape[0]
    w_both = twice(wts)

    lanes = lax.broadcasted_iota(jnp.int32, (ndir * K, width), 1)
    lanes2 = lax.broadcasted_iota(jnp.int32, (2 * ndir * K, width), 1)
    nd = ndir * K

    def products(jobs):
        both = [twice(x) for x, _, _ in jobs]
        tops = [mm(b, w, dims) for b, (_, w, dims) in zip(both, jobs)]
        return [t[:t.shape[0] // 2] + t[t.shape[0] // 2:] for t in tops]

    def frame_steps(table, place, gs):
        tabs = [stacked(jnp.concatenate([table[:, place[g]].reshape(rows, width), pad], axis=0), 0) for g in gs]
        pairs = [mm(w_both, jnp.concatenate(tabs[i:i + 2], axis=1), PLAIN) for i in range(0, len(gs), 2)]
        tops = [pairs[i // 2][:, i % 2 * width:(i % 2 + 1) * width] for i in range(len(gs))]
        jobs = []
        for g, top in zip(gs, tops):
            mix = top[:n_all] + top[n_all:]
            for d in range(ndir):
                x = jnp.concatenate([mix[d * K:(d + 1) * K], mix[nd + d * K:nd + (d + 1) * K]], axis=0)
                jobs.append((x, rot_by[d, g], PLAIN))
        ys = products(jobs)
        for i, g in enumerate(gs):
            y = ys[i * ndir:(i + 1) * ndir]
            frames[g] = pltpu.roll(jnp.concatenate([t[:K] for t in y] + [t[K:] for t in y], axis=0), 64, 1)

    def move_steps(gs):
        jobs = []
        for g in gs:
            x = jnp.where(lanes2 < 64, frames[(g - 1) % nblk], frames[g])
            jobs.append((x[:nd], tr_by[g], PLAIN))
            jobs.append((x[nd:], tr_back[g], BACK))
        ys = products(jobs)
        for i, g in enumerate(gs):
            moved[g] = pltpu.roll(ys[2 * i] + ys[2 * i + 1], 64, 1)

    def field_steps(gs):
        jobs = []
        for g in gs:
            u = jnp.where(lanes < 64, moved[g], moved[(g + 1) % nblk])
            for d in range(ndir):
                jobs.append((u[d * K:(d + 1) * K], rot_back[d, g], BACK))
        ys = products(jobs)
        for i, g in enumerate(gs):
            acc = ys[i * ndir]
            for d in range(1, ndir):
                acc = acc + ys[i * ndir + d]
            fieldb[g] = acc * mie[g:g + 1, :]

    def field_of(table, place, blocks_in, plan, before, after):
        have_f, have_u, have_h = set(), set(), set()
        for i, new in enumerate(blocks_in):
            before(i)
            frame_steps(table, place, new)
            have_f |= set(new)
            for step in plan[i][1]:
                run(step)
            ready = [g for g in range(nblk) if g not in have_u and g in have_f and (g - 1) % nblk in have_f]
            move_steps(ready)
            have_u |= set(ready)
            for step in plan[i][2]:
                run(step)
            ready = [g for g in range(nblk) if g not in have_h and g in have_u and (g + 1) % nblk in have_u]
            field_steps(ready)
            have_h |= set(ready)
            after(i, have_h)

    def line_start(source, sums, send, recv, axis):
        here, size = (row, groups) if axis == 0 else (col, blocks)
        for j in range(1, size):
            peer = lax.rem(here + j, size)
            pltpu.make_async_remote_copy(
                src_ref=source, dst_ref=sums.at[here], send_sem=send.at[0], recv_sem=recv.at[0],
                device_id=(peer, col) if axis == 0 else (row, peer), device_id_type=MESH,
            ).start()

    def line_all(sums, send, recv):
        many = pl.ds(0, sums.shape[0] - 1)
        return pltpu.make_async_remote_copy(
            src_ref=sums.at[many], dst_ref=sums.at[many], send_sem=send.at[0], recv_sem=recv.at[0],
            device_id=(lax.rem(row + 1, groups), col), device_id_type=MESH,
        )

    def second_line():
        line_all(gsum, gs, gr).wait_recv()
        line_all(gsum, gs, gr).wait_send()
        line = gsum[0]
        for j in range(1, groups):
            line = line + gsum[j]
        part2[...] = line
        bsum[col] = line
        line_start(part2, bsum, bs, br, 1)

    sums_in = [jnp.zeros((K, width), F32), jnp.zeros((K, width), F32)]

    def before1(i):
        if i:
            for step in plan1[i][0]:
                run(step)

    def after1(i, have):
        assert set(second_blocks[i]) <= have
        for g in second_blocks[i]:
            h = fieldb[g]
            hc[g] = h
            scaled = h * counts
            table2[mid, at2[g]] = scaled
            sums_in[0] = sums_in[0] + h * table1[mid, at1[g]]
            sums_in[1] = sums_in[1] + h * scaled
        if i == parts - 1:
            fold = lambda t: jnp.sum(t, axis=0, keepdims=True)
            zero = jnp.zeros((K - 3, width), F32)
            three = jnp.concatenate([fold(squares), fold(sums_in[0]), fold(sums_in[1]), zero], axis=0)
            three = three + pltpu.roll(three, 64, 1)
            three = three + pltpu.roll(three, 32, 1)
            lane1 = lax.broadcasted_iota(I32, (1, width), 1)
            mine_part = jnp.where(lane1 < 32, three[0:1], jnp.where(lane1 < 64, three[1:2], three[2:3]))
            part[...] = mine_part
            gsum[row] = mine_part
            line_start(part, gsum, gs, gr, 0)
        start_chunk(table2, chunks2[i], i, send2, recv2)

    field_of(table1, at1, first_blocks, plan1, before1, after1)

    def before2(i):
        for step in plan2[i][0]:
            run(step)

    field_of(table2, at2, second_blocks, plan2, before2, lambda i, have: None)

    line_all(bsum, bs, br).wait_recv()
    line_all(bsum, bs, br).wait_send()
    sums = bsum[0]
    for j in range(1, blocks):
        sums = sums + bsum[j]
    third = lax.broadcasted_iota(I32, (1, width), 1) // 32
    s_, a_, b_ = [jnp.sum(jnp.where(third == n, sums, 0.0), axis=1, keepdims=True) for n in range(3)]
    shift = entries * EPS
    q = (a_ + shift) / (s_ + shift)
    scale2 = (s_ + shift) / entries
    norm2 = (q * q * s_ - 2.0 * q * a_ + b_) / (entries * scale2) + EPS
    inv = 1.0 / jnp.sqrt(scale2 * norm2)
    for g in range(nblk):
        span = slice(g * width, (g + 1) * width)
        h = hc[g]
        coef[:K, span] = h * inv
        coef[K:, span] = (q * h - fieldb[g]) * inv
    factor[...] = jnp.broadcast_to(q * inv, factor.shape)


def closing(coef, factor, rhs, member, basis, image):
    spheres, full = rhs.shape
    mem = (lax.broadcasted_iota(I32, (K_DEV, spheres), 0) == member[...]).astype(BF16)
    mem3 = jnp.concatenate([mem.astype(F32)] * 3, axis=0).astype(BF16)
    scale = factor[0:1, 0:1]
    dims = (((0,), (0,)), ((), ()))

    def spread(x):
        return mm(mem3, thirds(x), dims)

    out = rhs[...] * scale - spread(coef[:K_DEV, :])
    basis[...] = out
    image[...] = out - spread(coef[K_DEV:, :])


def body(rhs, membership, pair_ends, pair_dir, pair_reach, pair_count, send_idx, rotation, translation, mie):
    groups, blocks = lax.axis_size("grp"), lax.axis_size("blk")
    spheres, full = rhs.shape
    ndir, nblk, width = rotation.shape[:3]
    npeer, cap = send_idx.shape[1:]
    npairs = pair_dir.shape[0]
    K = K_DEV
    vm = pl.BlockSpec(memory_space=pltpu.VMEM)
    hb = pl.BlockSpec(memory_space=pl.ANY)
    V, D = pltpu.VMEM, pltpu.SemaphoreType.DMA
    out = jax.ShapeDtypeStruct(rhs.shape, F32)
    entries = float(groups * blocks * spheres * full)
    parts = pl.pallas_call(
        functools.partial(kernel, groups, blocks, ndir, nblk, entries),
        out_shape=(V((2 * K, full), F32), V((K, width), F32), V(rhs.shape, F32), V((1, spheres), I32)),
        in_specs=[hb] * 5 + [pl.BlockSpec(memory_space=pltpu.SMEM)] + [hb] * 4,
        out_specs=(vm,) * 4,
        scratch_shapes=[
            V((2, npairs), I32), V((1, npairs), I32), V((1, npairs), F32), V((cap, npeer), I32), V((nblk, width), F32),
            V(rotation.shape, F32), V(translation.shape, F32),
            V((ndir, nblk, 2 * width, width), BF16), V((ndir, nblk, 2 * width, width), BF16),
            V((nblk, 2 * width, width), BF16), V((nblk, 2 * width, width), BF16),
            V((npeer + 1, nblk + ndir // 2 + 1, K, width), F32), V((npeer + 1, nblk, K, width), F32),
            V((nblk, 2 * ndir * K, width), F32), V((nblk, ndir * K, width), F32), V((nblk, K, width), F32),
            V((nblk, K, width), F32), V((1, width), F32), V((1, width), F32), V((groups, 1, width), F32), V((blocks, 1, width), F32),
            D((9,)), D((2, 3)), D((2, 3)), D((2, 3)), D((2, 3)),
            D((1,)), D((1,)), D((1,)), D((1,)),
        ],
        compiler_params=pltpu.CompilerParams(
            collective_id=0, has_side_effects=True, vmem_limit_bytes=48 << 20
        ),
    )(*[x if x.size == 1 else pltpu.with_memory_space_constraint(x, pltpu.HBM) for x in (
        rhs, membership[None, :], pair_ends.T, pair_dir[None, :], pair_reach[None, :], pair_count,
        send_idx[0].T, mie.reshape(nblk, width), rotation, translation,
    )])
    return pl.pallas_call(
        closing,
        out_shape=(out, out),
        in_specs=[vm] * 4,
        out_specs=(vm, vm),
        compiler_params=pltpu.CompilerParams(vmem_limit_bytes=8 << 20),
    )(*parts)


def solution(mesh):
    both = ("grp", "blk")
    placed = (
        P(both, None), P(both), P(both, None), P(both), P(both), P(both), P(both, None, None), P(), P(), P(),
    )
    return jax.shard_map(
        body, mesh=mesh, in_specs=placed, out_specs=(P(both, None), P(both, None)), check_vma=False
    )
```

```python
import functools

import jax
import jax.numpy as jnp
from jax import lax
from jax.experimental import pallas as pl
from jax.experimental.pallas import tpu as pltpu
from jax.sharding import PartitionSpec as P

K_DEV = 8
MESH = pl.DeviceIdType.MESH
F32 = jnp.float32
I32 = jnp.int32
BF16 = jnp.bfloat16
LAST = (((1,), (1,)), ((), ()))
PLAIN = (((1,), (0,)), ((), ()))
BACK = PLAIN
EPS = 1e-6


def mm(a, b, dims):
    return lax.dot_general(a, b, dims, preferred_element_type=F32)


def stacked(x, axis):
    hi = x.astype(BF16).astype(F32)
    return jnp.concatenate([hi, x - hi], axis=axis).astype(BF16)


def thirds(x):
    hi = x.astype(BF16).astype(F32)
    mid = (x - hi).astype(BF16).astype(F32)
    return jnp.concatenate([hi, mid, x - hi - mid], axis=0).astype(BF16)


def twice(x):
    both = stacked(x, 0)
    return jnp.concatenate([both, both], axis=1)


def offsets():
    out = []
    for f in range(15):
        if f != 7:
            out.append((f // 5 - 1, f % 5 - 2))
    return out


def kernel(
    groups, blocks, ndir, nblk, entries,
    rhs_hbm, member_hbm, ends_hbm, dir_hbm, reach_hbm, count, sent_hbm, mie_hbm, rot_hbm, trans_hbm,
    coef, factor, rhs, member,
    ends, dirs, reach, sent, mie,
    rot, trans, rot_by, rot_back, tr_by, tr_back, table1, table2, frames, moved, fieldb,
    hc, part, part2, gsum, bsum,
    wsem, send1, recv1, send2, recv2, gs, gr, bs, br,
):
    row = lax.axis_index("grp")
    col = lax.axis_index("blk")
    offs = offsets()
    npeer = len(offs)
    spheres = rhs.shape[0]
    width = 128
    K = K_DEV

    loads = [
        pltpu.make_async_copy(src, dst, wsem.at[i])
        for i, (src, dst) in enumerate([
            (rhs_hbm, rhs), (member_hbm, member), (ends_hbm, ends), (dir_hbm, dirs), (reach_hbm, reach),
            (sent_hbm, sent), (mie_hbm, mie), (rot_hbm, rot), (trans_hbm, trans),
        ])
    ]
    for load in loads[:7]:
        load.start()

    partner = 1 - 2 * lax.rem(row, 2)
    other = -partner

    beside = (row + other >= 0) & (row + other < groups)
    near = (-2, 2, -1, 1)

    def valid(dc):
        return ((col + dc >= 0) & (col + dc < blocks)).astype(I32)

    barrier = pltpu.get_barrier_semaphore()
    distance = max(2, blocks - 1 - 4)
    for j in range(1, groups):
        pl.semaphore_signal(barrier, inc=1, device_id=(lax.rem(row + j, groups), col), device_id_type=MESH)
    for dc in [d for d in range(-distance, distance + 1) if d]:
        v = valid(dc)
        pl.semaphore_signal(barrier, inc=1, device_id=(row + partner * (1 - v), col + dc * v), device_id_type=MESH)

    @pl.when(beside)
    def _():
        for dc in near:
            pl.semaphore_signal(barrier, inc=1, device_id=(row + other, col + dc * valid(dc)), device_id_type=MESH)

    cap = sent.shape[0]
    mid = npeer // 2
    for load in loads[:7]:
        load.wait()
    for load in loads[7:]:
        load.start()
    mem = (lax.broadcasted_iota(jnp.int32, (K, spheres), 0) == member[...]).astype(F32)
    agg = mm(jnp.concatenate([mem] * 3, axis=1).astype(BF16), thirds(rhs[...]), PLAIN)
    lead = ndir // 2 + 1
    for g in range(nblk):
        table1[mid, lead + g] = agg[:, g * width:(g + 1) * width]
    npairs = ends.shape[1]
    live = lax.broadcasted_iota(jnp.int32, (1, npairs), 1) < count[0]
    weight = jnp.where(live, reach[...], 0.0)
    key = dirs[...] * K + ends[0:1, :]
    left = jnp.where(lax.broadcasted_iota(jnp.int32, (ndir * K, npairs), 0) == key, weight, 0.0)
    right = (lax.broadcasted_iota(jnp.int32, (width, npairs), 0) == ends[1:2, :]).astype(F32).astype(BF16)
    own_w = mm(thirds(left), right, LAST)
    own_w = own_w[:ndir * K] + own_w[ndir * K:2 * ndir * K] + own_w[2 * ndir * K:]
    at = lax.broadcasted_iota(jnp.int32, (npeer, width), 1) - (64 + K)
    peer_row = lax.broadcasted_iota(jnp.int32, (npeer, width), 0) * cap
    spread_k = jnp.where((at >= peer_row) & (at < peer_row + cap), 1.0, 0.0)
    wide = mm(sent[...].astype(F32).astype(BF16), spread_k.astype(BF16), PLAIN)
    at4 = lax.broadcasted_iota(jnp.int32, (cap, width), 1) % cap
    row4 = lax.broadcasted_iota(jnp.int32, (cap, width), 0)
    ids = jnp.sum(jnp.where(at4 == (row4 + 64 + K) % cap, wide, 0.0), axis=0, keepdims=True)
    packed = [own_w[d * K:(d + 1) * K] for d in range(ndir)] + [jnp.broadcast_to(ids, (K, width))]
    for t in range(lead):
        second = packed[2 * t + 1]
        table1[mid, t] = packed[2 * t] + (second if 2 * t + 1 == ndir else pltpu.roll(second, 64, 1))

    @pl.when(jnp.logical_not(beside))
    def _():
        empty = pl.ds(5 * (1 - other), 5)
        table1[empty] = jnp.zeros((5,) + table1.shape[1:], F32)
        table2[empty] = jnp.zeros((5,) + table2.shape[1:], F32)

    pl.semaphore_wait(barrier, groups - 1 + 2 * distance + len(near) * beside.astype(I32))

    def copy(table, chunk, i, way, src, dst, send, recv, to_row, to_col):
        tiles = pl.ds(chunk[0], chunk[1] - chunk[0])
        return pltpu.make_async_remote_copy(
            src_ref=table.at[src, tiles], dst_ref=table.at[dst, tiles], send_sem=send.at[i, way], recv_sem=recv.at[i, way],
            device_id=(to_row, to_col), device_id_type=MESH,
        )

    def start_chunk(table, chunk, i, send, recv):
        for dc in near:
            v = valid(dc)
            copy(table, chunk, i, 0, mid, mid + dc * (2 * v - 1), send, recv, row + partner * (1 - v), col + dc * v).start()

        @pl.when(beside)
        def _():
            for dc in near + (0,):
                v = valid(dc)
                at = 5 * (1 + other) + 2 + dc * (2 * v - 1)
                copy(table, chunk, i, 2, mid, at, send, recv, row + other, col + dc * v).start()

    def whole(table, chunk, i, way, send, recv):
        many = pl.ds(0, (len(near), 5, 5)[way])
        return copy(table, chunk, i, way, many, many, send, recv, row + partner, col)

    def wait_send(table, chunk, i, send, recv):
        whole(table, chunk, i, 0, send, recv).wait_send()
        whole(table, chunk, i, 1, send, recv).wait_send()

        @pl.when(beside)
        def _():
            whole(table, chunk, i, 2, send, recv).wait_send()

    def pass_on(table, chunks, i, send, recv):
        whole(table, chunks[i], i, 0, send, recv).wait_recv()
        copy(table, chunks[i], i, 1, pl.ds(5, 5), pl.ds(5 * (1 + partner), 5), send, recv, row + partner, col).start()

    def wait_rest(table, chunks, i, send, recv):
        whole(table, chunks[i], i, 1, send, recv).wait_recv()

        @pl.when(beside)
        def _():
            whole(table, chunks[i], i, 2, send, recv).wait_recv()

    cuts = [0] + [nblk * c // 15 for c in (8,)] + [nblk]
    parts = len(cuts) - 1
    first_blocks = [list(range(a, b)) for a, b in zip(cuts, cuts[1:])]
    second_blocks = [list(range(max(a - 1, 1), b - 1)) for a, b in zip(cuts, cuts[1:])]
    second_blocks[-1] += [nblk - 1, 0]

    def spans(groups_of, lead):
        out, pos = [], 0
        for blocks_of in groups_of:
            end = pos + len(blocks_of) + (lead if not out else 0)
            out.append((pos, end))
            pos = end
        return out

    chunks1, chunks2 = spans(first_blocks, lead), spans(second_blocks, 0)
    at1 = {g: g + lead for g in range(nblk)}
    at2 = {g: (g - 1) % nblk for g in range(nblk)}
    plan1 = [[[(0, 0, 0), (0, 0, 1), (1, 0, 0)], [], []], [[(1, 0, 1)], [], []]]
    plan2 = [[[(0, 1, 0), (2, 0, 0), (1, 1, 0)], [(0, 1, 1)], []], [[(3, 0, 0), (3, 0, 1), (3, 1, 0), (3, 1, 1), (1, 1, 1)], [], []]]

    def run(step):
        act, which, j = step
        table, chunks, send, recv = ((table1, chunks1, send1, recv1), (table2, chunks2, send2, recv2))[which]
        if act == 0:
            pass_on(table, chunks, j, send, recv)
        elif act == 1:
            wait_rest(table, chunks, j, send, recv)
        elif act == 2:
            second_line()
        else:
            wait_send(table, chunks[j], j, send, recv)

    for i, chunk in enumerate(chunks1):
        start_chunk(table1, chunk, i, send1, recv1)

    squares = jnp.zeros((K, width), F32)
    for g in range(nblk):
        for s in range(0, spheres, K):
            v = rhs[s:s + K, g * width:(g + 1) * width]
            squares = squares + v * v
    counts = jnp.sum(mem, axis=1, keepdims=True)
    for load in loads[7:]:
        load.wait()
    for g in range(nblk):
        for d in range(ndir):
            rot_by[d, g] = stacked(rot[d, g], 0)
            rot_back[d, g] = stacked(rot[d, g].T, 0)
        tr_by[g] = stacked(trans[g], 0)
        tr_back[g] = stacked(trans[g].T, 0)
    for step in plan1[0][0]:
        run(step)

    rows = (npeer + 1) * K
    lane = lax.broadcasted_iota(jnp.int32, (width, width), 1)
    sub = lax.broadcasted_iota(jnp.int32, (width, width), 0)
    slot = sub // K
    from_row, from_col = row + 1 - slot // 5, col + 2 - slot % 5
    there = (slot <= npeer) & (from_row >= 0) & (from_row < groups) & (from_col >= 0) & (from_col < blocks)
    peer = jnp.where(slot > mid, slot - 1, slot)
    lane8 = lax.broadcasted_iota(jnp.int32, (K, width), 1)
    far = jnp.zeros((K, width), F32)
    for k in range(npeer):
        first = 64 + K + cap * k
        far = far + jnp.where((lane8 >= first) & (lane8 < first + cap), table1[k + (k >= mid), lead - 1], 0.0)
    far = pltpu.roll(far, 64, 1)
    far = jnp.broadcast_to(far[0:1], (width, width))
    low = K + cap * peer
    subk = (sub % K)
    wanted = jnp.where(lane < K, subk.astype(F32), far)
    lane_key = jnp.where(lane < K, lane.astype(F32), subk.astype(F32))
    begin = jnp.where(slot == mid, 0, low)
    end = jnp.where(slot == mid, K, low + cap)
    pick = jnp.where(there & (lane >= begin) & (lane < end) & (wanted == lane_key), 1.0, 0.0).astype(BF16)
    mine = pltpu.roll(jnp.broadcast_to(ids, (K, width)), 64, 1)
    sub8 = lax.broadcasted_iota(jnp.int32, (K, width), 0)
    named = jnp.where(lane8 < K, lane8.astype(F32), mine)
    take = jnp.where((lane8 < 64) & (named == sub8.astype(F32)), 1.0, 0.0).astype(BF16)
    back = K + cap * (npeer - 1 - peer)
    start = jnp.where(slot == mid, 0, back)
    stop = jnp.where(slot == mid, K, back + cap)
    keep = there & (lane >= start) & (lane < stop)
    front_w, behind_w = [], []
    pad = jnp.zeros((width - rows, width), F32)
    for d in range(ndir):
        halved = lambda t: pltpu.roll(t, 64, 1) if d % 2 else t
        owned = jnp.where(lane8 < 64, halved(table1[mid, d // 2]), 0.0)
        picked = mm(thirds(owned), pick, LAST)
        front_w.append(picked[:K] + picked[K:2 * K] + picked[2 * K:])
        every = jnp.where(keep, halved(jnp.concatenate([table1[:, d // 2].reshape(rows, width), pad], axis=0)), 0.0)
        taken = mm(take, thirds(every), LAST)
        behind_w.append(taken[:, :width] + taken[:, width:2 * width] + taken[:, 2 * width:])
    wts = jnp.concatenate(front_w + behind_w, axis=0)
    n_all = wts.shape[0]
    w_both = twice(wts)

    lanes = lax.broadcasted_iota(jnp.int32, (ndir * K, width), 1)
    lanes2 = lax.broadcasted_iota(jnp.int32, (2 * ndir * K, width), 1)
    nd = ndir * K

    def products(jobs):
        both = [twice(x) for x, _, _ in jobs]
        tops = [mm(b, w, dims) for b, (_, w, dims) in zip(both, jobs)]
        return [t[:t.shape[0] // 2] + t[t.shape[0] // 2:] for t in tops]

    def frame_steps(table, place, gs):
        tabs = [stacked(jnp.concatenate([table[:, place[g]].reshape(rows, width), pad], axis=0), 0) for g in gs]
        pairs = [mm(w_both, jnp.concatenate(tabs[i:i + 2], axis=1), PLAIN) for i in range(0, len(gs), 2)]
        tops = [pairs[i // 2][:, i % 2 * width:(i % 2 + 1) * width] for i in range(len(gs))]
        jobs = []
        for g, top in zip(gs, tops):
            mix = top[:n_all] + top[n_all:]
            for d in range(ndir):
                x = jnp.concatenate([mix[d * K:(d + 1) * K], mix[nd + d * K:nd + (d + 1) * K]], axis=0)
                jobs.append((x, rot_by[d, g], PLAIN))
        ys = products(jobs)
        for i, g in enumerate(gs):
            y = ys[i * ndir:(i + 1) * ndir]
            frames[g] = pltpu.roll(jnp.concatenate([t[:K] for t in y] + [t[K:] for t in y], axis=0), 64, 1)

    def move_steps(gs):
        jobs = []
        for g in gs:
            x = jnp.where(lanes2 < 64, frames[(g - 1) % nblk], frames[g])
            jobs.append((x[:nd], tr_by[g], PLAIN))
            jobs.append((x[nd:], tr_back[g], BACK))
        ys = products(jobs)
        for i, g in enumerate(gs):
            moved[g] = pltpu.roll(ys[2 * i] + ys[2 * i + 1], 64, 1)

    def field_steps(gs):
        jobs = []
        for g in gs:
            u = jnp.where(lanes < 64, moved[g], moved[(g + 1) % nblk])
            for d in range(ndir):
                jobs.append((u[d * K:(d + 1) * K], rot_back[d, g], BACK))
        ys = products(jobs)
        for i, g in enumerate(gs):
            acc = ys[i * ndir]
            for d in range(1, ndir):
                acc = acc + ys[i * ndir + d]
            fieldb[g] = acc * mie[g:g + 1, :]

    def field_of(table, place, blocks_in, plan, before, after):
        have_f, have_u, have_h = set(), set(), set()
        for i, new in enumerate(blocks_in):
            before(i)
            frame_steps(table, place, new)
            have_f |= set(new)
            for step in plan[i][1]:
                run(step)
            ready = [g for g in range(nblk) if g not in have_u and g in have_f and (g - 1) % nblk in have_f]
            move_steps(ready)
            have_u |= set(ready)
            for step in plan[i][2]:
                run(step)
            ready = [g for g in range(nblk) if g not in have_h and g in have_u and (g + 1) % nblk in have_u]
            field_steps(ready)
            have_h |= set(ready)
            after(i, have_h)

    def line_start(source, sums, send, recv, axis):
        here, size = (row, groups) if axis == 0 else (col, blocks)
        for j in range(1, size):
            peer = lax.rem(here + j, size)
            pltpu.make_async_remote_copy(
                src_ref=source, dst_ref=sums.at[here], send_sem=send.at[0], recv_sem=recv.at[0],
                device_id=(peer, col) if axis == 0 else (row, peer), device_id_type=MESH,
            ).start()

    def line_all(sums, send, recv):
        many = pl.ds(0, sums.shape[0] - 1)
        return pltpu.make_async_remote_copy(
            src_ref=sums.at[many], dst_ref=sums.at[many], send_sem=send.at[0], recv_sem=recv.at[0],
            device_id=(lax.rem(row + 1, groups), col), device_id_type=MESH,
        )

    def second_line():
        line_all(gsum, gs, gr).wait_recv()
        line_all(gsum, gs, gr).wait_send()
        line = gsum[0]
        for j in range(1, groups):
            line = line + gsum[j]
        part2[...] = line
        bsum[col] = line
        line_start(part2, bsum, bs, br, 1)

    sums_in = [jnp.zeros((K, width), F32), jnp.zeros((K, width), F32)]

    def before1(i):
        if i:
            for step in plan1[i][0]:
                run(step)

    def after1(i, have):
        assert set(second_blocks[i]) <= have
        for g in second_blocks[i]:
            h = fieldb[g]
            hc[g] = h
            scaled = h * counts
            table2[mid, at2[g]] = scaled
            sums_in[0] = sums_in[0] + h * table1[mid, at1[g]]
            sums_in[1] = sums_in[1] + h * scaled
        if i == parts - 1:
            fold = lambda t: jnp.sum(t, axis=0, keepdims=True)
            zero = jnp.zeros((K - 3, width), F32)
            three = jnp.concatenate([fold(squares), fold(sums_in[0]), fold(sums_in[1]), zero], axis=0)
            three = three + pltpu.roll(three, 64, 1)
            three = three + pltpu.roll(three, 32, 1)
            lane1 = lax.broadcasted_iota(I32, (1, width), 1)
            mine_part = jnp.where(lane1 < 32, three[0:1], jnp.where(lane1 < 64, three[1:2], three[2:3]))
            part[...] = mine_part
            gsum[row] = mine_part
            line_start(part, gsum, gs, gr, 0)
        start_chunk(table2, chunks2[i], i, send2, recv2)

    field_of(table1, at1, first_blocks, plan1, before1, after1)

    def before2(i):
        for step in plan2[i][0]:
            run(step)

    field_of(table2, at2, second_blocks, plan2, before2, lambda i, have: None)

    line_all(bsum, bs, br).wait_recv()
    line_all(bsum, bs, br).wait_send()
    sums = bsum[0]
    for j in range(1, blocks):
        sums = sums + bsum[j]
    third = lax.broadcasted_iota(I32, (1, width), 1) // 32
    s_, a_, b_ = [jnp.sum(jnp.where(third == n, sums, 0.0), axis=1, keepdims=True) for n in range(3)]
    shift = entries * EPS
    q = (a_ + shift) / (s_ + shift)
    scale2 = (s_ + shift) / entries
    norm2 = (q * q * s_ - 2.0 * q * a_ + b_) / (entries * scale2) + EPS
    inv = 1.0 / jnp.sqrt(scale2 * norm2)
    for g in range(nblk):
        span = slice(g * width, (g + 1) * width)
        h = hc[g]
        coef[:K, span] = h * inv
        coef[K:, span] = (q * h - fieldb[g]) * inv
    factor[...] = jnp.broadcast_to(q * inv, factor.shape)


def closing(coef, factor, rhs, member, basis, image):
    spheres, full = rhs.shape
    mem = (lax.broadcasted_iota(I32, (K_DEV, spheres), 0) == member[...]).astype(BF16)
    mem3 = jnp.concatenate([mem.astype(F32)] * 3, axis=0).astype(BF16)
    scale = factor[0:1, 0:1]
    dims = (((0,), (0,)), ((), ()))

    def spread(x):
        return mm(mem3, thirds(x), dims)

    out = rhs[...] * scale - spread(coef[:K_DEV, :])
    basis[...] = out
    image[...] = out - spread(coef[K_DEV:, :])


def body(rhs, membership, pair_ends, pair_dir, pair_reach, pair_count, send_idx, rotation, translation, mie):
    groups, blocks = lax.axis_size("grp"), lax.axis_size("blk")
    spheres, full = rhs.shape
    ndir, nblk, width = rotation.shape[:3]
    npeer, cap = send_idx.shape[1:]
    npairs = pair_dir.shape[0]
    K = K_DEV
    vm = pl.BlockSpec(memory_space=pltpu.VMEM)
    hb = pl.BlockSpec(memory_space=pl.ANY)
    V, D = pltpu.VMEM, pltpu.SemaphoreType.DMA
    out = jax.ShapeDtypeStruct(rhs.shape, F32)
    entries = float(groups * blocks * spheres * full)
    parts = pl.pallas_call(
        functools.partial(kernel, groups, blocks, ndir, nblk, entries),
        out_shape=(V((2 * K, full), F32), V((K, width), F32), V(rhs.shape, F32), V((1, spheres), I32)),
        in_specs=[hb] * 5 + [pl.BlockSpec(memory_space=pltpu.SMEM)] + [hb] * 4,
        out_specs=(vm,) * 4,
        scratch_shapes=[
            V((2, npairs), I32), V((1, npairs), I32), V((1, npairs), F32), V((cap, npeer), I32), V((nblk, width), F32),
            V(rotation.shape, F32), V(translation.shape, F32),
            V((ndir, nblk, 2 * width, width), BF16), V((ndir, nblk, 2 * width, width), BF16),
            V((nblk, 2 * width, width), BF16), V((nblk, 2 * width, width), BF16),
            V((npeer + 1, nblk + ndir // 2 + 1, K, width), F32), V((npeer + 1, nblk, K, width), F32),
            V((nblk, 2 * ndir * K, width), F32), V((nblk, ndir * K, width), F32), V((nblk, K, width), F32),
            V((nblk, K, width), F32), V((1, width), F32), V((1, width), F32), V((groups, 1, width), F32), V((blocks, 1, width), F32),
            D((9,)), D((2, 3)), D((2, 3)), D((2, 3)), D((2, 3)),
            D((1,)), D((1,)), D((1,)), D((1,)),
        ],
        compiler_params=pltpu.CompilerParams(
            collective_id=0, has_side_effects=True, vmem_limit_bytes=48 << 20
        ),
    )(*[x if x.size == 1 else pltpu.with_memory_space_constraint(x, pltpu.HBM) for x in (
        rhs, membership[None, :], pair_ends.T, pair_dir[None, :], pair_reach[None, :], pair_count,
        send_idx[0].T, mie.reshape(nblk, width), rotation, translation,
    )])
    return pl.pallas_call(
        closing,
        out_shape=(out, out),
        in_specs=[vm] * 4,
        out_specs=(vm, vm),
        compiler_params=pltpu.CompilerParams(vmem_limit_bytes=8 << 20),
    )(*parts)


def solution(mesh):
    both = ("grp", "blk")
    placed = (
        P(both, None), P(both), P(both, None), P(both), P(both), P(both), P(both, None, None), P(), P(), P(),
    )
    return jax.shard_map(
        body, mesh=mesh, in_specs=placed, out_specs=(P(both, None), P(both, None)), check_vma=False
    )
```
